256 devices in a mesh: ctx: 64 (over z_hi, x, y, core), ch: 4 (over z_lo).
Axes of the slice: x: 4, y: 4, z: 8 (z_hi: 2, z_lo: 4; z = z_hi * 4 + z_lo), core: 2. Of those that a mesh axis runs over, the one named last changes fastest.
Arguments:
- tokens: float32 [8192, 3072], P('ctx', 'ch'), may hold values from -6 to 6
- gate_input: float32 [8192, 3072], P('ctx', 'ch'), may hold values from -6 to 6
- cotangent: float32 [8192, 3072], P('ctx', 'ch'), may hold values from -6 to 6
- conv_weight: float32 [2, 4, 3072], P(None, None, 'ch'), may hold values from -3 to 3
- conv_bias: float32 [2, 3072], P(None, 'ch'), may hold values from -3 to 3
- select_weight: float32 [2, 3072, 128], P(None, 'ch'), may hold values from -0.109375 to 0.109375
- step_weight: float32 [2, 96, 3072], P(None, None, 'ch'), may hold values from -0.625 to 0.625
- step_bias: float32 [2, 3072], P(None, 'ch'), may hold values from -6 to -2.5
- decay_log: float32 [2, 16, 3072], P(None, None, 'ch'), may hold values from -12 to 2.75
- skip_gain: float32 [2, 3072], P(None, 'ch'), may hold values from 0.5 to 1.5
Outputs:
- block_out: float32 [8192, 3072], P('ctx', 'ch')
- tokens_grad: float32 [8192, 3072], P('ctx', 'ch')
- gate_grad: float32 [8192, 3072], P('ctx', 'ch')
- select_grad: float32 [2, 3072, 128], P(None, 'ch')
- step_grad: float32 [2, 96, 3072], P(None, None, 'ch')
The draws below stay inside these ranges and needn't reach their ends.
All inputs are finite; a program needn't handle non-finite values.
Results may differ from the reference program's by a relative error of at most 0.0003.
Values sent between devices are 32-bit elements; how exact they have to be, the bound alone decides.
A program may use at most 64 MiB of HBM per device.

```python
import jax
import jax.numpy as jnp
from jax import lax

E = 3072
N = 16
K = 4
R = 96
TOKENS = 8192
PROJ = 128


def block_levels(stream_key, shape, shards, smallest, top_value):
    gain, own = 1.0, jax.random.fold_in(stream_key, 6)
    for position, shards_of in shards:
        draws = jnp.exp(jax.random.uniform(jax.random.fold_in(own, position), (shards_of,), jnp.float32, smallest / len(shards), top_value / len(shards)))
        gain = gain * jnp.repeat(draws, shape[position] // shards_of).reshape([-1 if axis == position else 1 for axis in range(len(shape))])
    return gain


def scatter_about(own_key, shape, scale, reach, cuts=(), dtype=jnp.bfloat16):
    values = scale * jax.random.normal(own_key, shape, jnp.float32)
    if cuts:
        values = values * block_levels(own_key, shape, cuts, -0.22, 0.18)
    return jnp.clip(values, -reach, reach).astype(dtype)


def setup_inputs(seed: int = 0) -> dict:
    keys = jax.random.split(jax.random.key(seed), 11)
    tokens = scatter_about(keys[0], (TOKENS, E), 1.0, 6.0, ((0, 64), (1, 4)), jnp.float32)
    gate_input = scatter_about(keys[1], (TOKENS, E), 1.0, 6.0, ((0, 64), (1, 4)), jnp.float32)
    cotangent = scatter_about(keys[2], (TOKENS, E), 1.0, 6.0, ((0, 64), (1, 4)), jnp.float32)
    conv_weight = scatter_about(keys[3], (2, K, E), K ** -0.5, 3.0, ((2, 4),), jnp.float32)
    conv_bias = scatter_about(keys[4], (2, E), 0.5, 3.0, ((1, 4),), jnp.float32)
    select_weight = scatter_about(keys[5], (2, E, PROJ), E ** -0.5, 0.109375, ((1, 4),), jnp.float32)
    step_weight = scatter_about(keys[6], (2, R, E), R ** -0.5, 0.625, ((2, 4),), jnp.float32)
    step_bias = jnp.clip(-6.0 + 3.5 * jax.random.uniform(keys[7], (2, E), jnp.float32) ** block_levels(keys[7], (2, E), ((1, 4),), -0.2, 0.2), -6.0, -2.5)
    decay_log = jnp.clip(-12.0 + 14.75 * jax.random.uniform(keys[8], (2, N, E), jnp.float32) ** block_levels(keys[8], (2, N, E), ((2, 4),), -0.2, 0.2), -12.0, 2.75)
    skip_gain = jnp.clip(0.5 + 1.0 * jax.random.uniform(keys[9], (2, E), jnp.float32) ** block_levels(keys[9], (2, E), ((1, 4),), -0.2, 0.2), 0.5, 1.5)
    return dict(tokens=tokens, gate_input=gate_input, cotangent=cotangent, conv_weight=conv_weight, conv_bias=conv_bias, select_weight=select_weight, step_weight=step_weight, step_bias=step_bias, decay_log=decay_log, skip_gain=skip_gain)


def link(earlier, later):
    return (earlier[0] * later[0], later[0] * earlier[1] + later[1])

def selective(step, activated, in_basis, out_basis, rates):
    length, width = step.shape
    block = 256 if width % 256 == 0 else width
    count = width // block
    step_blocks = step.reshape(length, count, block).transpose(1, 0, 2)
    act_blocks = activated.reshape(length, count, block).transpose(1, 0, 2)
    rate_blocks = rates.reshape(rates.shape[0], count, block).transpose(1, 0, 2)

    def one_block(items):
        step_part, act_part, rate_part = items

        def advance(state, row):
            step_row, act_row, in_row, out_row = row
            state = jnp.exp(step_row[None, :] * rate_part) * state + in_row[:, None] * (step_row * act_row)[None, :]
            return (state, lax.optimization_barrier(jnp.sum(out_row[:, None] * state, axis=0)))
        start = jnp.zeros(rate_part.shape, jnp.float32)
        _, outputs = lax.scan(advance, start, (step_part, act_part, in_basis, out_basis))
        return outputs
    outputs = lax.map(jax.checkpoint(one_block), (step_blocks, act_blocks, rate_blocks))
    return outputs.transpose(1, 0, 2).reshape(length, width)

def branch(sequence, taps_weight, taps_bias, select_side, step_side, bias_side, decay_side, skip_side):
    length = sequence.shape[0]
    taps = taps_weight.shape[0]
    padded = jnp.concatenate([jnp.zeros((taps - 1, sequence.shape[1]), jnp.float32), sequence], 0)
    conv_pre = taps_bias[None, :]
    for lag in range(taps):
        conv_pre = conv_pre + taps_weight[lag][None, :] * padded[lag:lag + length]
    activated = jax.nn.silu(conv_pre)
    projection = jnp.dot(activated, select_side, precision=lax.Precision.HIGHEST, preferred_element_type=jnp.float32)
    low_rank = projection[:, :R]
    in_basis = projection[:, R:R + N]
    out_basis = projection[:, R + N:]
    step = jax.nn.softplus(jnp.dot(low_rank, step_side, precision=lax.Precision.HIGHEST, preferred_element_type=jnp.float32) + bias_side[None, :])
    rates = -jnp.exp(decay_side)
    return selective(step, activated, in_basis, out_basis, rates) + skip_side[None, :] * activated

def reference(tokens, gate_input, cotangent, conv_weight, conv_bias, select_weight, step_weight, step_bias, decay_log, skip_gain):

    def block(sequence, gate_values, select_all, step_all):
        forward_out = branch(sequence, conv_weight[0], conv_bias[0], select_all[0], step_all[0], step_bias[0], decay_log[0], skip_gain[0])
        backward_out = branch(jnp.flip(sequence, 0), conv_weight[1], conv_bias[1], select_all[1], step_all[1], step_bias[1], decay_log[1], skip_gain[1])
        return (forward_out + jnp.flip(backward_out, 0)) * jax.nn.silu(gate_values)
    block_out, pullback = jax.vjp(block, tokens, gate_input, select_weight, step_weight)
    tokens_grad, gate_grad, select_grad, step_grad = pullback(cotangent)
    return (block_out, tokens_grad, gate_grad, select_grad, step_grad)
```

```python
import jax
import jax.numpy as jnp
from jax import lax
from jax.experimental import pallas as pl
from jax.experimental.pallas import tpu as pltpu
from jax.sharding import PartitionSpec as P

F32 = jnp.float32
HIGH = lax.Precision.HIGHEST
MESH = pl.DeviceIdType.MESH

T = 128
C = 8
L = 16
E = 768
N = 16
R = 96
W = 128
B = E // W
TILES = 64

VM = pl.BlockSpec(memory_space=pltpu.VMEM)


def sds(*shape):
    return jax.ShapeDtypeStruct(shape, F32)


def sigmoid(v):
    return 1.0 / (1.0 + jnp.exp(-v))


def softplus(v):
    return jnp.maximum(v, 0.0) + jnp.log1p(jnp.exp(-jnp.abs(v)))


def rows8(i):
    return pl.ds(pl.multiple_of(i * 8, 8), 8)


def nn(a, b):
    return lax.dot_general(a, b, (((1,), (0,)), ((), ())), precision=HIGH, preferred_element_type=F32)


def nt(a, b):
    return lax.dot_general(a, b, (((1,), (1,)), ((), ())), precision=HIGH, preferred_element_type=F32)


def tn(a, b):
    return lax.dot_general(a, b, (((0,), (0,)), ((), ())), precision=HIGH, preferred_element_type=F32)


class Links:
    def __init__(self, send, recv):
        self.send, self.recv, self.used = send, recv, 0
        self.all = []

    def start(self, src, dst, device):
        k = self.used
        self.used += 1
        copy = pltpu.make_async_remote_copy(
            src_ref=src,
            dst_ref=dst,
            send_sem=self.send.at[k],
            recv_sem=self.recv.at[k],
            device_id=device,
            device_id_type=MESH,
        )
        copy.start()
        self.all.append(copy)
        return copy

    def finish(self):
        for copy in self.all:
            copy.wait_send()


def arrived(copies):
    for copy in copies:
        copy.wait_recv()


def greet(devices):
    barrier = pltpu.get_barrier_semaphore()
    for device in devices:
        pl.semaphore_signal(barrier, inc=1, device_id=device, device_id_type=MESH)
    pl.semaphore_wait(barrier, len(devices))


def plus(a, p, n):
    return lax.rem(a + p, n)


def fill_edges(ext, prev, nxt, has_prev, has_next):
    sub = lax.broadcasted_iota(jnp.int32, (C, E), 0)
    for k in range(3):
        last = ext[3 + L - 3 + k]
        row = jnp.broadcast_to(prev[k : k + 1], (C, E))
        row = jnp.where(has_prev, row, 0.0)
        ext[k] = jnp.where(sub == 0, row, pltpu.roll(last, 1, 0))
        first = ext[3 + k]
        row = jnp.broadcast_to(nxt[k : k + 1], (C, E))
        row = jnp.where(has_next, row, 0.0)
        ext[3 + L + k] = jnp.where(sub == C - 1, row, pltpu.roll(first, C - 1, 0))


def sum_over_ch(links, part, landed, own, total, me, ctx):
    sends = []
    for p in range(1, 4):
        peer = plus(me, p, 4)
        sends.append(links.start(part.at[pl.ds(pl.multiple_of(peer * 64, 64), 64)], landed.at[p - 1], (ctx, peer)))

    def middle():
        arrived(sends)
        mine = pl.ds(pl.multiple_of(me * 64, 64), 64)
        value = part[mine] + landed[0] + landed[1] + landed[2]
        own[...] = value
        total[mine] = value
        return [links.start(own, total.at[mine], (ctx, plus(me, p, 4))) for p in range(1, 4)]

    return middle


def by_lanes(src, dst):
    for b in range(B):
        dst[b] = src[:, b * W : (b + 1) * W]


def every(i):
    return pl.ds(i, C, stride=L)


def front_kernel(tok, cw, cb, sw, act_o, sg_o, proj_o, ext, tiles, prev, nxt, part, landed, own, total, send, recv):
    ctx, me = lax.axis_index("ctx"), lax.axis_index("ch")
    after, before = plus(ctx, 1, TILES), plus(ctx, TILES - 1, TILES)
    greet([(after, me), (before, me)] + [(ctx, plus(me, p, 4)) for p in range(1, 4)])
    links = Links(send, recv)
    halo = [
        links.start(tok.at[pl.ds(T - 8, 8)], prev, (after, me)),
        links.start(tok.at[pl.ds(0, 8)], nxt, (before, me)),
    ]
    by_lanes(tok, tiles)
    for i in range(L):
        for b in range(B):
            ext[3 + i, :, b * W : (b + 1) * W] = tiles[b, every(i)]
    arrived(halo)
    fill_edges(ext, prev[5:8], nxt[0:3], ctx > 0, ctx < TILES - 1)

    def conv(i, carry):
        for d in range(2):
            v = jnp.broadcast_to(cb[d : d + 1], (C, E))
            for k in range(4):
                v = v + cw[d, k : k + 1] * ext[i + (k if d == 0 else 6 - k)]
            s = sigmoid(v)
            act_o[d, rows8(i)] = v * s
            sg_o[d, rows8(i)] = s * (1.0 + v * (1.0 - s))
        return carry

    lax.fori_loop(0, L, conv, 0)
    for d in range(2):
        part[d * T : (d + 1) * T] = nn(act_o[d], sw[d])
    gathers = sum_over_ch(links, part, landed, own, total, me, ctx)()
    arrived(gathers)
    for d in range(2):
        proj_o[d] = total[d * T : (d + 1) * T]
    links.finish()


def front(tok, cw, cb, sw):
    return pl.pallas_call(
        front_kernel,
        out_shape=(sds(2, T, E), sds(2, T, E), sds(2, T, W)),
        in_specs=[VM] * 4,
        out_specs=(VM,) * 3,
        scratch_shapes=[
            pltpu.VMEM((L + 6, C, E), F32),
            pltpu.VMEM((B, T, W), F32),
            pltpu.VMEM((8, E), F32),
            pltpu.VMEM((8, E), F32),
            pltpu.VMEM((2 * T, W), F32),
            pltpu.VMEM((3, 64, W), F32),
            pltpu.VMEM((64, W), F32),
            pltpu.VMEM((2 * T, W), F32),
            pltpu.SemaphoreType.DMA((8,)),
            pltpu.SemaphoreType.DMA((8,)),
        ],
        compiler_params=pltpu.CompilerParams(collective_id=0, has_side_effects=True, vmem_limit_bytes=32 << 20),
        name="front",
    )(tok, cw, cb, sw)


def spread_bases(proj, inb, outb):
    def one(i, carry):
        for d in range(2):
            block = proj[d, rows8(i)]
            for n in range(N):
                inb[d, i, n] = jnp.broadcast_to(block[:, R + n : R + n + 1], (C, W))
                outb[d, i, n] = jnp.broadcast_to(block[:, R + N + n : R + N + n + 1], (C, W))
        return carry

    lax.fori_loop(0, L, one, 0)


def gated(gate, cot, g, i):
    for b in range(B):
        v = gate[b, every(i)]
        g[rows8(i), b * W : (b + 1) * W] = cot[b, every(i)] * v * sigmoid(v)


def local_kernel(
    proj, act, gate, cot, stw, stb, dl, pre_o, step_o, g_o, cu, cd, cp, msg, inb, outb, drv, gates, cots
):
    by_lanes(gate, gates)
    by_lanes(cot, cots)
    for d in range(2):
        pre_o[d] = nn(proj[d][:, :R], stw[d]) + stb[d : d + 1]

    def prepare(i, carry):
        gated(gates, cots, g_o, i)
        for d in range(2):
            st = softplus(pre_o[d, rows8(i)])
            step_o[d, rows8(i)] = st
            drv[d, rows8(i)] = st * act[d, rows8(i)]
        return carry

    lax.fori_loop(0, L, prepare, 0)
    spread_bases(proj, inb, outb)
    H = 8
    for d in range(2):
        for half in range(N // H):

            def block(c, carry, d=d, half=half):
                lanes = pl.ds(pl.multiple_of(c * W, W), W)
                rate = [
                    jnp.broadcast_to(-jnp.exp(dl[d, half * H + j : half * H + j + 1, lanes]), (C, W)) for j in range(H)
                ]

                def advance(i, state):
                    f, p, a = state
                    ii = i if d == 0 else L - 1 - i
                    st, dr = step_o[d, rows8(ii), lanes], drv[d, rows8(ii), lanes]
                    gg = g_o[rows8(ii), lanes]
                    nf, np_, na = [], [], []
                    for j in range(H):
                        dec = jnp.exp(st * rate[j])
                        nf.append(dec * f[j] + inb[d, ii, half * H + j] * dr)
                        q = p[j] * dec
                        np_.append(q)
                        na.append(a[j] + q * (outb[d, ii, half * H + j] * gg))
                    return nf, np_, na

                zero = [jnp.zeros((C, W), F32)] * H
                f, p, a = lax.fori_loop(0, L, advance, (zero, [jnp.ones((C, W), F32)] * H, zero))
                up, down = (cu, cd) if d == 0 else (cd, cu)
                for j in range(H):
                    n = half * H + j
                    row = rows8(d * 12 + (n % 2) * B + c)
                    up[n // 2, row] = f[j]
                    cp[n // 2, row] = p[j]
                    down[n // 2, row] = a[j]
                return carry

            lax.fori_loop(0, B, block, 0)

    def totals(q, carry):
        for k in range(3):
            u = dn = jnp.zeros((C, W), F32)
            pt = jnp.ones((C, W), F32)
            for s in range(C):
                at = pl.ds(k * 64 + s, C, stride=C)
                p = cp[q, at]
                u = p * u + cu[q, at]
                pt = pt * p
                back = pl.ds(k * 64 + C - 1 - s, C, stride=C)
                dn = cp[q, back] * dn + cd[q, back]
            msg[q, k * 8 : k * 8 + 8] = u
            msg[q, 24 + k * 8 : 32 + k * 8] = dn
            msg[q, 48 + k * 8 : 56 + k * 8] = pt
        return carry

    lax.fori_loop(0, 8, totals, 0)


def local(proj, act, gate, cot, stw, stb, dl):
    return pl.pallas_call(
        local_kernel,
        out_shape=(
            sds(2, T, E),
            sds(2, T, E),
            sds(T, E),
            sds(8, 192, W),
            sds(8, 192, W),
            sds(8, 192, W),
            sds(8, 72, W),
        ),
        in_specs=[VM] * 7,
        out_specs=(VM,) * 7,
        scratch_shapes=[
            pltpu.VMEM((2, L, N, C, W), F32),
            pltpu.VMEM((2, L, N, C, W), F32),
            pltpu.VMEM((2, T, E), F32),
            pltpu.VMEM((B, T, W), F32),
            pltpu.VMEM((B, T, W), F32),
        ],
        compiler_params=pltpu.CompilerParams(vmem_limit_bytes=32 << 20),
        name="local",
    )(proj, act, gate, cot, stw, stb, dl)


def carry_kernel(msg, car_o, r1, tot, r2, zs, zr, out, rc, send, recv):
    ctx, ch = lax.axis_index("ctx"), lax.axis_index("ch")
    q, x, z = lax.rem(ctx, 8), lax.rem(ctx // 8, 4), ctx // 32
    base = ctx - q
    xbase = z * 32 + q
    partner = lax.rem(ctx + 32, TILES)
    near = [plus(q, p, 8) for p in range(1, 8)]
    across = [plus(x, p, 4) for p in range(1, 4)]
    greet([(base + k, ch) for k in near] + [(xbase + k * 8, ch) for k in across] + [(partner, ch)])
    links = Links(send, recv)
    copies = [links.start(msg.at[k], r1.at[q], (base + k, ch)) for k in near]
    r1[q] = msg[q]
    arrived(copies)

    def fold(buf, count, u, dn):
        pt = None
        for s in range(count):
            u = buf[s, 48:72] * u + buf[s, 0:24]
            b = count - 1 - s
            dn = buf[b, 48:72] * dn + buf[b, 24:48]
            pt = buf[s, 48:72] if pt is None else pt * buf[s, 48:72]
        return u, dn, pt

    zero = jnp.zeros((24, W), F32)
    u, dn, pt = fold(r1, 8, zero, zero)
    tot[0:24], tot[24:48], tot[48:72] = u, dn, pt
    copies = [links.start(tot, r2.at[x], (xbase + k * 8, ch)) for k in across]
    r2[x] = tot[...]
    arrived(copies)
    u, dn, pt = fold(r2, 4, zero, zero)
    zs[...] = jnp.where(z == 0, u, dn)
    copies = [links.start(zs, zr, (partner, ch))]
    arrived(copies)
    got = zr[...]
    u, dn = jnp.where(z == 1, got, 0.0), jnp.where(z == 0, got, 0.0)
    for s in range(4):
        u = jnp.where(s < x, r2[s, 48:72] * u + r2[s, 0:24], u)
        b = 3 - s
        dn = jnp.where(b > x, r2[b, 48:72] * dn + r2[b, 24:48], dn)
    for s in range(8):
        out[s, 0:24] = u
        u = r1[s, 48:72] * u + r1[s, 0:24]
        b = 7 - s
        out[b, 24:48] = dn
        dn = r1[b, 48:72] * dn + r1[b, 24:48]
    copies = [links.start(out.at[k], rc.at[q], (base + k, ch)) for k in near]
    rc[q] = out[q]
    arrived(copies)
    car_o[...] = rc[...]
    links.finish()


def carries(msg):
    return pl.pallas_call(
        carry_kernel,
        out_shape=sds(8, 48, W),
        in_specs=[VM],
        out_specs=VM,
        scratch_shapes=[
            pltpu.VMEM((8, 72, W), F32),
            pltpu.VMEM((72, W), F32),
            pltpu.VMEM((4, 72, W), F32),
            pltpu.VMEM((24, W), F32),
            pltpu.VMEM((24, W), F32),
            pltpu.VMEM((8, 48, W), F32),
            pltpu.VMEM((8, 48, W), F32),
            pltpu.SemaphoreType.DMA((18,)),
            pltpu.SemaphoreType.DMA((18,)),
        ],
        compiler_params=pltpu.CompilerParams(collective_id=1, has_side_effects=True, vmem_limit_bytes=16 << 20),
        name="carries",
    )(msg)


def sweep_kernel(
    proj, act, gate, cot, stw, dl, skip, pre, step, g, cu, cd, cp, car,
    out_o, gg_o, ga_o, pg_o, sp_o,
    inb, outb, drv, rt, su, sd, ss, go, gi, ya, dg, stt, wpad, gates, cots,
):
    by_lanes(gate, gates)
    by_lanes(cot, cots)
    def starts(q, carry):
        for k in range(3):
            u, dn = car[q, k * 8 : k * 8 + 8], car[q, 24 + k * 8 : 32 + k * 8]
            for s in range(C):
                at = pl.ds(k * 64 + s, C, stride=C)
                su[q, at] = u
                u = cp[q, at] * u + cu[q, at]
                back = pl.ds(k * 64 + C - 1 - s, C, stride=C)
                sd[q, back] = dn
                dn = cp[q, back] * dn + cd[q, back]
        return carry

    lax.fori_loop(0, 8, starts, 0)
    spread_bases(proj, inb, outb)
    for d in range(2):
        for n in range(N):
            rt[d, n] = jnp.broadcast_to(-jnp.exp(dl[d, n : n + 1]), (C, E))

    def prepare(i, carry):
        y = jnp.zeros((C, E), F32)
        for d in range(2):
            a = act[d, rows8(i)]
            drv[d, rows8(i)] = step[d, rows8(i)] * a
            y = y + skip[d : d + 1] * a
        ya[rows8(i)] = y
        return carry

    lax.fori_loop(0, L, prepare, 0)
    H, Q = 8, 3
    QW = Q * W

    def folded(v):
        r = v[:, :W]
        for k in range(1, Q):
            r = r + v[:, k * W : (k + 1) * W]
        return r

    def wide(v):
        return jnp.concatenate([v] * Q, axis=1)

    for d in range(2):
        fs, as_ = (su, sd) if d == 0 else (sd, su)
        for half in range(N // H):
            for cb in range(B // Q):
                lanes = pl.ds(cb * QW, QW)

                def begin(src, j, d=d, half=half, cb=cb):
                    n = half * H + j
                    row = d * 12 + (n % 2) * B + cb * Q
                    return jnp.concatenate([src[n // 2, pl.ds((row + k) * 8, 8)] for k in range(Q)], axis=1)

                def forward(i, state, d=d, half=half, cb=cb, lanes=lanes):
                    ii = i if d == 0 else L - 1 - i
                    st, dr = step[d, rows8(ii), lanes], drv[d, rows8(ii), lanes]
                    gg = g[rows8(ii), lanes]
                    y = ya[rows8(ii), lanes]
                    new = []
                    for j in range(H):
                        n = half * H + j
                        s = jnp.exp(st * rt[d, n, :, lanes]) * state[j] + wide(inb[d, ii, n]) * dr
                        y = y + wide(outb[d, ii, n]) * s
                        v = folded(s * gg)
                        go[d, ii, n] = v if cb == 0 else go[d, ii, n] + v
                        ss[i + 1, j] = s
                        new.append(s)
                    ya[rows8(ii), lanes] = y
                    return new

                first = [begin(fs, j) for j in range(H)]
                for j in range(H):
                    ss[0, j] = first[j]
                lax.fori_loop(0, L, forward, first)

                def retreat(t, carried, d=d, half=half, cb=cb, lanes=lanes):
                    i = L - 1 - t
                    ii = i if d == 0 else L - 1 - i
                    st, dr = step[d, rows8(ii), lanes], drv[d, rows8(ii), lanes]
                    gg = g[rows8(ii), lanes]
                    if half == 0:
                        a1 = a2 = jnp.zeros((C, QW), F32)
                    else:
                        a1, a2 = stt[d, rows8(ii), lanes], dg[d, rows8(ii), lanes]
                    new = []
                    for j in range(H):
                        n = half * H + j
                        rate = rt[d, n, :, lanes]
                        adj = carried[j] + wide(outb[d, ii, n]) * gg
                        back = jnp.exp(st * rate) * adj
                        a1 = a1 + (back * ss[i, j]) * rate
                        a2 = a2 + adj * wide(inb[d, ii, n])
                        v = folded(adj * dr)
                        gi[d, ii, n] = v if cb == 0 else gi[d, ii, n] + v
                        new.append(back)
                    stt[d, rows8(ii), lanes] = a1
                    dg[d, rows8(ii), lanes] = a2
                    return new

                lax.fori_loop(0, L, retreat, [begin(as_, j) for j in range(H)])

    def close(i, carry):
        at = rows8(i)
        for b in range(B):
            v, ct, y = gates[b, every(i)], cots[b, every(i)], ya[at, b * W : (b + 1) * W]
            s = sigmoid(v)
            gates[b, every(i)] = y * v * s
            cots[b, every(i)] = ct * y * (s * (1.0 + v * (1.0 - s)))
        for d in range(2):
            slope = dg[d, at]
            ga_o[d, at] = g[at] * skip[d : d + 1] + slope * step[d, at]
            stt[d, at] = (stt[d, at] + slope * act[d, at]) * sigmoid(pre[d, at])
        return carry

    lax.fori_loop(0, L, close, 0)
    for b in range(B):
        out_o[:, b * W : (b + 1) * W] = gates[b]
        gg_o[:, b * W : (b + 1) * W] = cots[b]
    wpad[...] = jnp.zeros_like(wpad)
    lane = lax.broadcasted_iota(jnp.int32, (C, W), 1)
    for d in range(2):
        wpad[d, 0:R] = stw[d]
        sp_o[d] = tn(proj[d], stt[d])[:R]
        pg_o[d] = nt(stt[d], wpad[d])

    def bases(i, carry):
        for d in range(2):
            v = pg_o[d, rows8(i)]
            for n in range(N):
                v = v + jnp.where(lane == R + n, jnp.sum(gi[d, i, n], axis=1, keepdims=True), 0.0)
                v = v + jnp.where(lane == R + N + n, jnp.sum(go[d, i, n], axis=1, keepdims=True), 0.0)
            pg_o[d, rows8(i)] = v
        return carry

    lax.fori_loop(0, L, bases, 0)


def sweep(*args):
    return pl.pallas_call(
        sweep_kernel,
        out_shape=(sds(T, E), sds(T, E), sds(2, T, E), sds(2, T, W), sds(2, R, E)),
        in_specs=[VM] * 14,
        out_specs=(VM,) * 5,
        scratch_shapes=[
            pltpu.VMEM((2, L, N, C, W), F32),
            pltpu.VMEM((2, L, N, C, W), F32),
            pltpu.VMEM((2, T, E), F32),
            pltpu.VMEM((2, N, C, E), F32),
            pltpu.VMEM((8, 192, W), F32),
            pltpu.VMEM((8, 192, W), F32),
            pltpu.VMEM((L + 1, 8, C, 3 * W), F32),
            pltpu.VMEM((2, L, N, C, W), F32),
            pltpu.VMEM((2, L, N, C, W), F32),
            pltpu.VMEM((T, E), F32),
            pltpu.VMEM((2, T, E), F32),
            pltpu.VMEM((2, T, E), F32),
            pltpu.VMEM((2, W, E), F32),
            pltpu.VMEM((B, T, W), F32),
            pltpu.VMEM((B, T, W), F32),
        ],
        compiler_params=pltpu.CompilerParams(vmem_limit_bytes=48 << 20),
        name="sweep",
    )(*args)


def back_kernel(
    pg, act, sg, ga, sw, cw, sp,
    tg_o, selg_o, stepg_o,
    landed, own, total, slp, ext0, ext1, send0, send1, prev, nxt, tgp, tiles,
    s_r0, s0, s_r1, s1, s_r2, s2, s_r3, s3, s_x, s_y, s_out,
    t_r0, t0, t_r1, t1, t_r2, t2, t_r3, t3, t_y, t_x, t_out,
    send, recv,
):
    ctx, me = lax.axis_index("ctx"), lax.axis_index("ch")
    after, before = plus(ctx, 1, TILES), plus(ctx, TILES - 1, TILES)
    core, y, x = lax.rem(ctx, 2), lax.rem(ctx // 2, 4), lax.rem(ctx // 8, 4)
    other = 1 - core
    mate = (ctx - core + other, me)
    far = (lax.rem(ctx + 32, TILES), me)
    ys = [plus(y, p, 4) for p in range(1, 4)]
    xs = [plus(x, p, 4) for p in range(1, 4)]
    ydev = [(ctx + (k - y) * 2, me) for k in ys]
    xdev = [(ctx + (k - x) * 8, me) for k in xs]
    greet([(after, me), (before, me), mate, far] + ydev + xdev + [(ctx, plus(me, p, 4)) for p in range(1, 4)])
    links = Links(send, recv)

    def rows(k, n):
        return pl.ds(pl.multiple_of(k * n, 8), n)

    def scatter(src, n, ks, devices, dst):
        return [links.start(src.at[rows(k, n)], dst.at[p], dev) for p, (k, dev) in enumerate(zip(ks, devices))]

    def summed(src, k, n, dst):
        return src[rows(k, n)] + dst[0] + dst[1] + dst[2]

    step_core = [links.start(sp.at[other], s_r0, mate)]
    middle = sum_over_ch(links, pg, landed, own, total, me, ctx)
    arrived(step_core)
    s0[...] = sp[core] + s_r0[...]
    step_y = scatter(s0, 24, ys, ydev, s_r1)
    gathers = middle()
    arrived(step_y)
    s1[0:24] = summed(s0, y, 24, s_r1)
    s1[24:32] = jnp.zeros((8, E), F32)
    step_x = scatter(s1, 8, xs, xdev, s_r2)
    arrived(gathers)
    for d in range(2):
        slp[d] = tn(act[d], total[d * T : (d + 1) * T])
    sel_core = [links.start(slp.at[other], t_r0, mate)]
    for d, ext in enumerate((ext0, ext1)):
        tgp[...] = nt(total[d * T : (d + 1) * T], sw[d])

        def conv_grad(i, carry, d=d, ext=ext):
            ext[3 + i] = (ga[d, rows8(i)] + tgp[rows8(i)]) * sg[d, rows8(i)]
            return carry

        lax.fori_loop(0, L, conv_grad, 0)
    for k in range(3):
        send0[k : k + 1] = ext0[3 + k, 0:1]
        send1[k : k + 1] = ext1[3 + L - 3 + k, C - 1 : C]
    halo = [links.start(send0, nxt, (before, me)), links.start(send1, prev, (after, me))]
    arrived(sel_core)
    t0[...] = slp[core] + t_r0[...]
    sel_x = scatter(t0, 192, xs, xdev, t_r1)
    arrived(step_x)
    s2[...] = summed(s1, x, 8, s_r2)
    step_z = [links.start(s2, s_r3, far)]
    arrived(halo)
    fill_edges(ext0, prev[0:3], nxt[0:3], ctx > 0, ctx < TILES - 1)
    fill_edges(ext1, prev[0:3], nxt[0:3], ctx > 0, ctx < TILES - 1)

    def conv_back(i, carry):
        v = jnp.zeros((C, E), F32)
        for k in range(4):
            v = v + cw[0, k : k + 1] * ext0[i + 6 - k] + cw[1, k : k + 1] * ext1[i + k]
        for b in range(B):
            tiles[b, every(i)] = v[:, b * W : (b + 1) * W]
        return carry

    lax.fori_loop(0, L, conv_back, 0)
    for b in range(B):
        tg_o[:, b * W : (b + 1) * W] = tiles[b]
    arrived(sel_x)
    t1[...] = summed(t0, x, 192, t_r1)
    sel_y = scatter(t1, 48, ys, ydev, t_r2)
    arrived(step_z)
    v = s2[...] + s_r3[...]
    s3[...] = v
    s_x[rows(x, 8)] = v
    step_x = [links.start(s3, s_x.at[rows(x, 8)], dev) for dev in xdev]
    arrived(sel_y)
    t2[...] = summed(t1, y, 48, t_r2)
    sel_z = [links.start(t2, t_r3, far)]
    arrived(step_x)
    s_y[rows(y, 24)] = s_x[0:24]
    step_y = [links.start(s_x.at[pl.ds(0, 24)], s_y.at[rows(y, 24)], dev) for dev in ydev]
    arrived(sel_z)
    v = t2[...] + t_r3[...]
    t3[...] = v
    t_y[rows(y, 48)] = v
    sel_y = [links.start(t3, t_y.at[rows(y, 48)], dev) for dev in ydev]
    arrived(step_y)
    step_core = [links.start(s_y, s_out, mate)]
    arrived(sel_y)
    t_x[rows(x, 192)] = t_y[...]
    sel_x = [links.start(t_y, t_x.at[rows(x, 192)], dev) for dev in xdev]
    stepg_o[core] = s_y[...]
    arrived(step_core)
    stepg_o[other] = s_out[...]
    arrived(sel_x)
    sel_core = [links.start(t_x, t_out, mate)]
    selg_o[core] = t_x[...]
    arrived(sel_core)
    selg_o[other] = t_out[...]
    links.finish()


def back(*args):
    v = lambda *shape: pltpu.VMEM(shape, F32)
    return pl.pallas_call(
        back_kernel,
        out_shape=(sds(T, E), sds(2, E, W), sds(2, R, E)),
        in_specs=[VM] * 7,
        out_specs=(VM,) * 3,
        scratch_shapes=[
            v(3, 64, W), v(64, W), v(2 * T, W), v(2, E, W), v(L + 6, C, E), v(L + 6, C, E),
            v(8, E), v(8, E), v(8, E), v(8, E), v(T, E), v(B, T, W),
            v(R, E), v(R, E), v(3, 24, E), v(32, E), v(3, 8, E), v(8, E), v(8, E), v(8, E), v(32, E), v(R, E), v(R, E),
            v(E, W), v(E, W), v(3, 192, W), v(192, W), v(3, 48, W), v(48, W), v(48, W), v(48, W), v(192, W), v(E, W),
            v(E, W),
            pltpu.SemaphoreType.DMA((38,)),
            pltpu.SemaphoreType.DMA((38,)),
        ],
        compiler_params=pltpu.CompilerParams(collective_id=2, has_side_effects=True, vmem_limit_bytes=40 << 20),
        name="back",
    )(*args)


def on_device(tok, gate, cot, cw, cb, sw, stw, stb, dl, skip):
    act, sg, proj = front(tok, cw, cb, sw)
    pre, step, g, cu, cd, cp, msg = local(proj, act, gate, cot, stw, stb, dl)
    car = carries(msg)
    out, gg, ga, pg, sp = sweep(proj, act, gate, cot, stw, dl, skip, pre, step, g, cu, cd, cp, car)
    tg, selg, stepg = back(pg.reshape(2 * T, W), act, sg, ga, sw, cw, sp)
    return out, tg, gg, selg, stepg


def solution(mesh):
    row = P("ctx", "ch")
    in_specs = (
        row,
        row,
        row,
        P(None, None, "ch"),
        P(None, "ch"),
        P(None, "ch", None),
        P(None, None, "ch"),
        P(None, "ch"),
        P(None, None, "ch"),
        P(None, "ch"),
    )
    out_specs = (row, row, row, P(None, "ch", None), P(None, None, "ch"))
    return jax.shard_map(on_device, mesh=mesh, in_specs=in_specs, out_specs=out_specs, check_vma=False)
```

```python
import jax
import jax.numpy as jnp
from jax import lax
from jax.experimental import pallas as pl
from jax.experimental.pallas import tpu as pltpu
from jax.sharding import PartitionSpec as P

F32 = jnp.float32
HIGH = lax.Precision.HIGHEST
MESH = pl.DeviceIdType.MESH

T = 128
C = 8
L = 16
E = 768
N = 16
R = 96
W = 128
B = E // W
TILES = 64

VM = pl.BlockSpec(memory_space=pltpu.VMEM)


def sds(*shape):
    return jax.ShapeDtypeStruct(shape, F32)


LOG2E = 1.4426950408889634
LN2 = 0.6931471805599453


def sigmoid(v):
    return 1.0 / (1.0 + jnp.exp(-v))


def softplus(v):
    return jnp.maximum(v, 0.0) + jnp.log1p(jnp.exp(-jnp.abs(v)))


def rows8(i):
    return pl.ds(pl.multiple_of(i * 8, 8), 8)


def nn(a, b):
    return lax.dot_general(a, b, (((1,), (0,)), ((), ())), precision=HIGH, preferred_element_type=F32)


def nt(a, b):
    return lax.dot_general(a, b, (((1,), (1,)), ((), ())), precision=HIGH, preferred_element_type=F32)


def tn(a, b):
    return lax.dot_general(a, b, (((0,), (0,)), ((), ())), precision=HIGH, preferred_element_type=F32)


class Links:
    def __init__(self, send, recv):
        self.send, self.recv, self.used = send, recv, 0
        self.all = []

    def start(self, src, dst, device):
        k = self.used
        self.used += 1
        copy = pltpu.make_async_remote_copy(
            src_ref=src,
            dst_ref=dst,
            send_sem=self.send.at[k],
            recv_sem=self.recv.at[k],
            device_id=device,
            device_id_type=MESH,
        )
        copy.start()
        self.all.append(copy)
        return copy

    def finish(self):
        for copy in self.all:
            copy.wait_send()


def arrived(copies):
    for copy in copies:
        copy.wait_recv()


def greet(devices):
    barrier = pltpu.get_barrier_semaphore()
    for device in devices:
        pl.semaphore_signal(barrier, inc=1, device_id=device, device_id_type=MESH)
    pl.semaphore_wait(barrier, len(devices))


def plus(a, p, n):
    return lax.rem(a + p, n)


def fill_edges(ext, prev, nxt, has_prev, has_next):
    sub = lax.broadcasted_iota(jnp.int32, (C, E), 0)
    for k in range(3):
        last = ext[3 + L - 3 + k]
        row = jnp.broadcast_to(prev[k : k + 1], (C, E))
        row = jnp.where(has_prev, row, 0.0)
        ext[k] = jnp.where(sub == 0, row, pltpu.roll(last, 1, 0))
        first = ext[3 + k]
        row = jnp.broadcast_to(nxt[k : k + 1], (C, E))
        row = jnp.where(has_next, row, 0.0)
        ext[3 + L + k] = jnp.where(sub == C - 1, row, pltpu.roll(first, C - 1, 0))


def by_lanes(src, dst):
    for b in range(B):
        dst[b] = src[:, b * W : (b + 1) * W]


def every(i):
    return pl.ds(i, C, stride=L)


def rows(k, n):
    return pl.ds(pl.multiple_of(k * n, 8), n)


class ChannelSum:
    def __init__(self, links, part, landed, own, total, me, ctx):
        self.links, self.part, self.landed, self.own, self.total = links, part, landed, own, total
        self.me, self.peers = me, [(ctx, plus(me, p, 4)) for p in range(1, 4)]

    def scatter(self):
        self.copies = [
            self.links.start(self.part.at[rows(peer[1], 32)], self.landed.at[p], peer)
            for p, peer in enumerate(self.peers)
        ]

    def gather(self):
        arrived(self.copies)
        mine = rows(self.me, 32)
        value = self.part[mine] + self.landed[0] + self.landed[1] + self.landed[2]
        self.own[...] = value
        self.total[mine] = value
        self.copies = [self.links.start(self.own, self.total.at[mine], peer) for peer in self.peers]

    def wait(self):
        arrived(self.copies)


class TileSum:
    def __init__(self, links, place, src, r0, t0, r1, t2, r3, t3, t4, fin):
        self.links, self.place, self.src = links, place, src
        self.r0, self.t0, self.r1, self.t2, self.r3, self.t3, self.t4, self.fin = r0, t0, r1, t2, r3, t3, t4, fin

    def core(self):
        self.copies = [self.links.start(self.src.at[rows(1 - self.place.core, 384)], self.r0, self.place.mate)]

    def scatter(self):
        arrived(self.copies)
        self.t0[...] = self.src[rows(self.place.core, 384)] + self.r0[...]
        self.copies = [
            self.links.start(self.t0.at[rows(k, 24)], self.r1.at[p], dev)
            for p, (k, dev) in enumerate(self.place.plane)
        ]

    def far(self):
        arrived(self.copies)
        v = self.t0[rows(self.place.k, 24)]
        for p in range(15):
            v = v + self.r1[p]
        self.t2[...] = v
        self.copies = [self.links.start(self.t2, self.r3, self.place.far)]

    def gather(self):
        arrived(self.copies)
        v = self.t2[...] + self.r3[...]
        mine = rows(self.place.k, 24)
        self.t3[...] = v
        self.t4[mine] = v
        self.copies = [self.links.start(self.t3, self.t4.at[mine], dev) for _, dev in self.place.plane]

    def join(self):
        arrived(self.copies)
        self.copies = [self.links.start(self.t4, self.fin, self.place.mate)]

    def end(self, write):
        write(self.place.core, self.t4)
        arrived(self.copies)
        write(1 - self.place.core, self.fin)


class Place:
    def __init__(self):
        ctx, me = lax.axis_index("ctx"), lax.axis_index("ch")
        self.ctx, self.me = ctx, me
        self.after, self.before = (plus(ctx, 1, TILES), me), (plus(ctx, TILES - 1, TILES), me)
        self.core, self.y, self.x = lax.rem(ctx, 2), lax.rem(ctx // 2, 4), lax.rem(ctx // 8, 4)
        self.q, self.z = lax.rem(ctx, 8), ctx // 32
        self.mate = (ctx - self.core + 1 - self.core, me)
        self.far = (lax.rem(ctx + 32, TILES), me)
        self.k = self.x * 4 + self.y
        self.plane = []
        for dx in range(4):
            for dy in range(4):
                if dx or dy:
                    x, y = plus(self.x, dx, 4), plus(self.y, dy, 4)
                    self.plane.append((x * 4 + y, (ctx + (x - self.x) * 8 + (y - self.y) * 2, me)))
        base = ctx - self.q
        self.near = [(k, (base + k, me)) for k in [plus(self.q, p, 8) for p in range(1, 8)]]
        self.across = [(ctx + (plus(self.x, p, 4) - self.x) * 8, me) for p in range(1, 4)]
        self.ch = [(ctx, plus(me, p, 4)) for p in range(1, 4)]

    def everyone(self):
        plane = [dev for _, dev in self.plane]
        return [self.after, self.before, self.far] + plane + [dev for _, dev in self.near] + self.ch


def exchange_carries(links, place, msg, r1, tot, r2, zs, zr, out, rc):
    q, x, z = place.q, place.x, place.z
    copies = [links.start(msg.at[k], r1.at[q], dev) for k, dev in place.near]
    r1[q] = msg[q]
    arrived(copies)

    def fold(buf, count, u, dn):
        pt = None
        for s in range(count):
            u = buf[s, 48:72] * u + buf[s, 0:24]
            b = count - 1 - s
            dn = buf[b, 48:72] * dn + buf[b, 24:48]
            pt = buf[s, 48:72] if pt is None else pt * buf[s, 48:72]
        return u, dn, pt

    zero = jnp.zeros((24, W), F32)
    u, dn, pt = fold(r1, 8, zero, zero)
    tot[0:24], tot[24:48], tot[48:72] = u, dn, pt
    copies = [links.start(tot, r2.at[x], dev) for dev in place.across]
    r2[x] = tot[...]
    arrived(copies)
    u, dn, pt = fold(r2, 4, zero, zero)
    zs[...] = jnp.where(z == 0, u, dn)
    arrived([links.start(zs, zr, place.far)])
    got = zr[...]
    u, dn = jnp.where(z == 1, got, 0.0), jnp.where(z == 0, got, 0.0)
    for s in range(4):
        u = jnp.where(s < x, r2[s, 48:72] * u + r2[s, 0:24], u)
        b = 3 - s
        dn = jnp.where(b > x, r2[b, 48:72] * dn + r2[b, 24:48], dn)
    for s in range(8):
        out[s, 0:24] = u
        u = r1[s, 48:72] * u + r1[s, 0:24]
        b = 7 - s
        out[b, 24:48] = dn
        dn = r1[b, 48:72] * dn + r1[b, 24:48]
    copies = [links.start(out.at[k], rc.at[q], dev) for k, dev in place.near]
    rc[q] = out[q]
    arrived(copies)


def block_kernel(
    tok_h, gate_h, cot_h, cw_h, cb_h, sw_h, stw_h, stb_h, dl_h, skip_h,
    out_o, tg_o, gg_o, selg_o, stepg_o,
    tok, gate, cot, cw, cb, sw, stw, stb, dl, skip, in_sem,
    tiles, gates, cots, prev, nxt, prev2, nxt2, send0, send1, ext0, ext1,
    act, sg, part, landed, own, proj, part2, landed2, own2, gp,
    pre, step, drv, g, rt, inb, outb, dec, cu, cd, cp, su, sd,
    msg, cr1, ctot, cr2, czs, czr, cout, crc,
    ss, go, gi, ya, dg, stt, wpad, tgp,
    w_src, w_r0, w_t0, w_r1, w_t2, w_r3, w_t3, w_t4, w_fin,
    send, recv,
):
    pairs = (
        (tok_h, tok), (cw_h, cw), (cb_h, cb), (sw_h, sw), (gate_h, gate), (cot_h, cot),
        (stw_h, stw), (stb_h, stb), (dl_h, dl), (skip_h, skip),
    )
    loads = [pltpu.make_async_copy(a, b, in_sem.at[k]) for k, (a, b) in enumerate(pairs)]
    for load in loads:
        load.start()
    place = Place()
    ctx, me = place.ctx, place.me
    greet(place.everyone())
    links = Links(send, recv)
    halo = [
        links.start(tok_h.at[pl.ds(T - 8, 8)], prev, place.after),
        links.start(tok_h.at[pl.ds(0, 8)], nxt, place.before),
    ]
    loads[0].wait()
    by_lanes(tok, tiles)
    for i in range(L):
        for b in range(B):
            ext0[3 + i, :, b * W : (b + 1) * W] = tiles[b, every(i)]
    for load in loads[1:4]:
        load.wait()
    arrived(halo)
    fill_edges(ext0, prev[5:8], nxt[0:3], ctx > 0, ctx < TILES - 1)
    sums = [ChannelSum(links, part.at[d], landed.at[d], own.at[d], proj.at[d], me, ctx) for d in range(2)]
    for d in range(2):

        def conv(i, carry, d=d):
            v = jnp.broadcast_to(cb[d : d + 1], (C, E))
            for k in range(4):
                v = v + cw[d, k : k + 1] * ext0[i + (k if d == 0 else 6 - k)]
            s = sigmoid(v)
            act[d, rows8(i)] = v * s
            sg[d, rows8(i)] = s * (1.0 + v * (1.0 - s))
            return carry

        lax.fori_loop(0, L, conv, 0)
        part[d] = nn(act[d], sw[d])
        sums[d].scatter()
    for load in loads[4:]:
        load.wait()
    by_lanes(gate, gates)
    by_lanes(cot, cots)

    def gated(i, carry):
        for b in range(B):
            v = gates[b, every(i)]
            g[rows8(i), b * W : (b + 1) * W] = cots[b, every(i)] * v * sigmoid(v)
        return carry

    lax.fori_loop(0, L, gated, 0)
    for d in range(2):
        for n in range(N):
            rt[d, n] = jnp.broadcast_to(-jnp.exp(dl[d, n : n + 1]) * LOG2E, (C, E))
    for d in range(2):
        sums[d].gather()
    H = 8
    for d in range(2):
        sums[d].wait()
        pre[d] = nn(proj[d][:, :R], stw[d]) + stb[d : d + 1]

        def prepare(i, carry, d=d):
            st = softplus(pre[d, rows8(i)])
            step[d, rows8(i)] = st
            drv[d, rows8(i)] = st * act[d, rows8(i)]
            block = proj[d, rows8(i)]
            for n in range(N):
                inb[d, i, n] = jnp.broadcast_to(block[:, R + n : R + n + 1], (C, W))
                outb[d, i, n] = jnp.broadcast_to(block[:, R + N + n : R + N + n + 1], (C, W))
            return carry

        lax.fori_loop(0, L, prepare, 0)
        up, down = (cu, cd) if d == 0 else (cd, cu)
        for half in range(N // H):

            def ends(c, carry, d=d, half=half, up=up, down=down):
                lanes = pl.ds(pl.multiple_of(c * W, W), W)

                def advance(i, state):
                    f, p, a = state
                    ii = i if d == 0 else L - 1 - i
                    st, dr = step[d, rows8(ii), lanes], drv[d, rows8(ii), lanes]
                    gg = g[rows8(ii), lanes]
                    nf, np_, na = [], [], []
                    for j in range(H):
                        n = half * H + j
                        e = jnp.exp2(st * rt[d, n, :, lanes])
                        dec[d, ii, n, :, lanes] = e
                        nf.append(e * f[j] + inb[d, ii, n] * dr)
                        v = p[j] * e
                        np_.append(v)
                        na.append(a[j] + v * (outb[d, ii, n] * gg))
                    return nf, np_, na

                zero = [jnp.zeros((C, W), F32)] * H
                f, p, a = lax.fori_loop(0, L, advance, (zero, [jnp.ones((C, W), F32)] * H, zero), unroll=UNROLL)
                for j in range(H):
                    n = half * H + j
                    row = rows8(d * 12 + (n % 2) * B + c)
                    up[n // 2, row] = f[j]
                    cp[n // 2, row] = p[j]
                    down[n // 2, row] = a[j]
                return carry

            lax.fori_loop(0, B, ends, 0)

    def totals(q, carry):
        for k in range(3):
            u = dn = jnp.zeros((C, W), F32)
            pt = jnp.ones((C, W), F32)
            for s in range(C):
                at = pl.ds(k * 64 + s, C, stride=C)
                p = cp[q, at]
                u = p * u + cu[q, at]
                pt = pt * p
                back = pl.ds(k * 64 + C - 1 - s, C, stride=C)
                dn = cp[q, back] * dn + cd[q, back]
            msg[q, k * 8 : k * 8 + 8] = u
            msg[q, 24 + k * 8 : 32 + k * 8] = dn
            msg[q, 48 + k * 8 : 56 + k * 8] = pt
        return carry

    lax.fori_loop(0, 8, totals, 0)
    exchange_carries(links, place, msg, cr1, ctot, cr2, czs, czr, cout, crc)

    def starts(q, carry):
        for k in range(3):
            u, dn = crc[q, k * 8 : k * 8 + 8], crc[q, 24 + k * 8 : 32 + k * 8]
            for s in range(C):
                at = pl.ds(k * 64 + s, C, stride=C)
                su[q, at] = u
                u = cp[q, at] * u + cu[q, at]
                back = pl.ds(k * 64 + C - 1 - s, C, stride=C)
                sd[q, back] = dn
                dn = cp[q, back] * dn + cd[q, back]
        return carry

    lax.fori_loop(0, 8, starts, 0)
    Q = 3
    QW = Q * W
    lane = lax.broadcasted_iota(jnp.int32, (C, W), 1)

    def folded(v):
        r = v[:, :W]
        for k in range(1, Q):
            r = r + v[:, k * W : (k + 1) * W]
        return r

    def wide(v):
        return jnp.concatenate([v] * Q, axis=1)

    def begin(src, d, half, cb, j):
        n = half * H + j
        row = d * 12 + (n % 2) * B + cb * Q
        return jnp.concatenate([src[n // 2, pl.ds((row + k) * 8, 8)] for k in range(Q)], axis=1)

    blocks = [(half, cb) for half in range(N // H) for cb in range(B // Q)]

    def sweep(d):
        fs, bs = (su, sd) if d == 0 else (sd, su)
        for half, cb in blocks:
            lanes = pl.ds(cb * QW, QW)

            def forward(i, state, half=half, cb=cb, lanes=lanes):
                ii = i if d == 0 else L - 1 - i
                dr, gg = drv[d, rows8(ii), lanes], g[rows8(ii), lanes]
                if half == 0:
                    y = skip[d : d + 1, lanes] * act[d, rows8(ii), lanes]
                    if d == 1:
                        y = y + ya[rows8(ii), lanes]
                else:
                    y = ya[rows8(ii), lanes]
                new = []
                for j in range(H):
                    n = half * H + j
                    s = dec[d, ii, n, :, lanes] * state[j] + wide(inb[d, ii, n]) * dr
                    y = y + wide(outb[d, ii, n]) * s
                    v = folded(s * gg)
                    go[ii, n] = v if cb == 0 else go[ii, n] + v
                    ss[i + 1, j] = s
                    new.append(s)
                ya[rows8(ii), lanes] = y
                return new

            first = [begin(fs, d, half, cb, j) for j in range(H)]
            for j in range(H):
                ss[0, j] = first[j]
            lax.fori_loop(0, L, forward, first)

            def retreat(t, carried, half=half, cb=cb, lanes=lanes):
                i = L - 1 - t
                ii = i if d == 0 else L - 1 - i
                dr, gg = drv[d, rows8(ii), lanes], g[rows8(ii), lanes]
                if half == 0:
                    a1 = a2 = jnp.zeros((C, QW), F32)
                else:
                    a1, a2 = stt[rows8(ii), lanes], dg[rows8(ii), lanes]
                new = []
                for j in range(H):
                    n = half * H + j
                    adj = carried[j] + wide(outb[d, ii, n]) * gg
                    back = dec[d, ii, n, :, lanes] * adj
                    a1 = a1 + (back * ss[i, j]) * rt[d, n, :, lanes]
                    a2 = a2 + adj * wide(inb[d, ii, n])
                    v = folded(adj * dr)
                    gi[ii, n] = v if cb == 0 else gi[ii, n] + v
                    new.append(back)
                stt[rows8(ii), lanes] = a1
                dg[rows8(ii), lanes] = a2
                return new

            lax.fori_loop(0, L, retreat, [begin(bs, d, half, cb, j) for j in range(H)])

        def close(i, carry):
            at = rows8(i)
            slope = dg[at]
            ga = g[at] * skip[d : d + 1] + slope * step[d, at]
            stt[at] = (stt[at] * LN2 + slope * act[d, at]) * sigmoid(pre[d, at])
            drv[d, at] = ga
            return carry

        lax.fori_loop(0, L, close, 0)
        wpad[0:R] = stw[d]
        part2[d] = nt(stt[...], wpad[...])

        def bases(i, carry):
            v = part2[d, rows8(i)]
            for n in range(N):
                v = v + jnp.where(lane == R + n, jnp.sum(gi[i, n], axis=1, keepdims=True), 0.0)
                v = v + jnp.where(lane == R + N + n, jnp.sum(go[i, n], axis=1, keepdims=True), 0.0)
            part2[d, rows8(i)] = v
            return carry

        lax.fori_loop(0, L, bases, 0)

    wpad[...] = jnp.zeros_like(wpad)
    back_sums = [ChannelSum(links, part2.at[d], landed2.at[d], own2.at[d], gp.at[d], me, ctx) for d in range(2)]
    weights = [
        TileSum(links, place, *[r.at[k] for r in (w_src, w_r0, w_t0, w_r1, w_t2, w_r3, w_t3, w_t4, w_fin)])
        for k in range(4)
    ]
    s0, s1, t0, t1 = weights

    def step_part(d, stream):
        v = tn(proj[d], stt[...])
        for b in range(B):
            stream.src[b * W : (b + 1) * W] = v[:, b * W : (b + 1) * W]

    def select_part(d, stream, ext):
        stream.src[...] = tn(act[d], gp[d])
        stream.core()
        tgp[...] = nt(gp[d], sw[d])

        def conv_grad(i, carry):
            ext[3 + i] = (drv[d, rows8(i)] + tgp[rows8(i)]) * sg[d, rows8(i)]
            return carry

        lax.fori_loop(0, L, conv_grad, 0)

    def step_end(d):
        def write(core, src):
            for b in range(3):
                lanes = pl.ds(pl.multiple_of(core * 384 + b * W, W), W)
                stepg_o[d, :, lanes] = src[b * W : b * W + R]

        return write

    def select_end(d):
        def write(core, src):
            selg_o[d, rows(core, 384)] = src[...]

        return write

    sweep(0)
    back_sums[0].scatter()
    step_part(0, s0)
    s0.core()
    sweep(1)
    back_sums[1].scatter()
    back_sums[0].gather()
    step_part(1, s1)
    s1.core()
    s0.scatter()
    back_sums[0].wait()
    select_part(0, t0, ext0)
    back_sums[1].gather()
    s0.far()
    s1.scatter()
    t0.scatter()
    back_sums[1].wait()
    select_part(1, t1, ext1)
    for k in range(3):
        send0[k : k + 1] = ext0[3 + k, 0:1]
        send1[k : k + 1] = ext1[3 + L - 3 + k, C - 1 : C]
    halo = [links.start(send0, nxt2, place.before), links.start(send1, prev2, place.after)]
    s0.gather()
    t1.scatter()
    s1.far()
    t0.far()

    def gates_back(i, carry):
        for b in range(B):
            v, ct, y = gates[b, every(i)], cots[b, every(i)], ya[rows8(i), b * W : (b + 1) * W]
            s = sigmoid(v)
            gates[b, every(i)] = y * v * s
            cots[b, every(i)] = ct * y * (s * (1.0 + v * (1.0 - s)))
        return carry

    lax.fori_loop(0, L, gates_back, 0)
    for b in range(B):
        out_o[:, b * W : (b + 1) * W] = gates[b]
        gg_o[:, b * W : (b + 1) * W] = cots[b]
    s0.join()
    t1.far()
    s1.gather()
    t0.gather()
    arrived(halo)
    fill_edges(ext0, prev2[0:3], nxt2[0:3], ctx > 0, ctx < TILES - 1)
    fill_edges(ext1, prev2[0:3], nxt2[0:3], ctx > 0, ctx < TILES - 1)

    def conv_back(i, carry):
        v = jnp.zeros((C, E), F32)
        for k in range(4):
            v = v + cw[0, k : k + 1] * ext0[i + 6 - k] + cw[1, k : k + 1] * ext1[i + k]
        for b in range(B):
            tiles[b, every(i)] = v[:, b * W : (b + 1) * W]
        return carry

    lax.fori_loop(0, L, conv_back, 0)
    for b in range(B):
        tg_o[:, b * W : (b + 1) * W] = tiles[b]
    t1.gather()
    s1.join()
    t0.join()
    s0.end(step_end(0))
    t1.join()
    s1.end(step_end(1))
    t0.end(select_end(0))
    t1.end(select_end(1))
    links.finish()


UNROLL = 2


def on_device(*args):
    v = lambda *shape: pltpu.VMEM(shape, F32)
    chunks = v(8, 192, W)
    copies = 2 + 12 + 18 + 12 + 2 + 4 * 33
    any_ = pl.BlockSpec(memory_space=pl.ANY)
    return pl.pallas_call(
        block_kernel,
        out_shape=(sds(T, E), sds(T, E), sds(T, E), sds(2, E, W), sds(2, R, E)),
        in_specs=[any_] * 10,
        out_specs=(VM,) * 5,
        scratch_shapes=[
            v(T, E), v(T, E), v(T, E), v(2, 4, E), v(2, E), v(2, E, W), v(2, R, E), v(2, E), v(2, N, E), v(2, E),
            pltpu.SemaphoreType.DMA((10,)),
            v(B, T, W), v(B, T, W), v(B, T, W), v(8, E), v(8, E), v(8, E), v(8, E), v(8, E), v(8, E),
            v(L + 6, C, E), v(L + 6, C, E),
            v(2, T, E), v(2, T, E), v(2, T, W), v(2, 3, 32, W), v(2, 32, W), v(2, T, W),
            v(2, T, W), v(2, 3, 32, W), v(2, 32, W), v(2, T, W),
            v(2, T, E), v(2, T, E), v(2, T, E), v(T, E), v(2, N, C, E), v(2, L, N, C, W), v(2, L, N, C, W),
            v(2, L, N, C, E), chunks, chunks, chunks, chunks, chunks,
            v(8, 72, W), v(8, 72, W), v(72, W), v(4, 72, W), v(24, W), v(24, W), v(8, 48, W), v(8, 48, W),
            v(L + 1, 8, C, 3 * W), v(L, N, C, W), v(L, N, C, W), v(T, E), v(T, E), v(T, E), v(W, E), v(T, E),
            v(4, E, W), v(4, 384, W), v(4, 384, W), v(4, 15, 24, W), v(4, 24, W), v(4, 24, W), v(4, 24, W),
            v(4, 384, W), v(4, 384, W),
            pltpu.SemaphoreType.DMA((copies,)),
            pltpu.SemaphoreType.DMA((copies,)),
        ],
        compiler_params=pltpu.CompilerParams(
            collective_id=0, has_side_effects=True, vmem_limit_bytes=60 << 20
        ),
        name="block",
    )(*args)


def solution(mesh):
    row = P("ctx", "ch")
    in_specs = (
        row,
        row,
        row,
        P(None, None, "ch"),
        P(None, "ch"),
        P(None, "ch", None),
        P(None, None, "ch"),
        P(None, "ch"),
        P(None, None, "ch"),
        P(None, "ch"),
    )
    out_specs = (row, row, row, P(None, "ch", None), P(None, None, "ch"))
    return jax.shard_map(on_device, mesh=mesh, in_specs=in_specs, out_specs=out_specs, check_vma=False)
```

```python
import jax
import jax.numpy as jnp
from jax import lax
from jax.experimental import pallas as pl
from jax.experimental.pallas import tpu as pltpu
from jax.sharding import PartitionSpec as P

F32 = jnp.float32
MESH = pl.DeviceIdType.MESH

T = 128
C = 8
L = 16
E = 768
N = 16
R = 96
W = 128
B = E // W
TILES = 64

VM = pl.BlockSpec(memory_space=pltpu.VMEM)


def sds(*shape):
    return jax.ShapeDtypeStruct(shape, F32)


LOG2E = 1.4426950408889634
LN2 = 0.6931471805599453


def sigmoid(v):
    return 1.0 / (1.0 + jnp.exp(-v))


def softplus(v):
    return jnp.maximum(v, 0.0) + jnp.log1p(jnp.exp(-jnp.abs(v)))


def rows8(i):
    return pl.ds(pl.multiple_of(i * 8, 8), 8)


def parts(a):
    high = a.astype(jnp.bfloat16)
    return high, (a - high.astype(F32)).astype(jnp.bfloat16)


def product(a, b, left, right):
    (ah, al), (bh, bl) = parts(a), parts(b)

    def dot(u, v):
        return lax.dot_general(u, v, (((left,), (right,)), ((), ())), preferred_element_type=F32)

    return dot(ah, bh) + (dot(ah, bl) + dot(al, bh))


def nn(a, b):
    return product(a, b, 1, 0)


def nt(a, b):
    return product(a, b, 1, 1)


def tn(a, b):
    return product(a, b, 0, 0)


class Links:
    def __init__(self, send, recv):
        self.send, self.recv, self.used = send, recv, 0
        self.all = []

    def start(self, src, dst, device):
        k = self.used
        self.used += 1
        copy = pltpu.make_async_remote_copy(
            src_ref=src,
            dst_ref=dst,
            send_sem=self.send.at[k],
            recv_sem=self.recv.at[k],
            device_id=device,
            device_id_type=MESH,
        )
        copy.start()
        self.all.append(copy)
        return copy

    def finish(self):
        for copy in self.all:
            copy.wait_send()


def arrived(copies):
    for copy in copies:
        copy.wait_recv()


def hail(devices):
    barrier = pltpu.get_barrier_semaphore()
    for device in devices:
        pl.semaphore_signal(barrier, inc=1, device_id=device, device_id_type=MESH)
    return lambda: pl.semaphore_wait(barrier, len(devices))


def plus(a, p, n):
    return lax.rem(a + p, n)


def fill_edges(ext, prev, nxt, has_prev, has_next):
    sub = lax.broadcasted_iota(jnp.int32, (C, E), 0)
    for k in range(3):
        last = ext[3 + L - 3 + k]
        row = jnp.broadcast_to(prev[k : k + 1], (C, E))
        row = jnp.where(has_prev, row, 0.0)
        ext[k] = jnp.where(sub == 0, row, pltpu.roll(last, 1, 0))
        first = ext[3 + k]
        row = jnp.broadcast_to(nxt[k : k + 1], (C, E))
        row = jnp.where(has_next, row, 0.0)
        ext[3 + L + k] = jnp.where(sub == C - 1, row, pltpu.roll(first, C - 1, 0))


def by_lanes(src, dst):
    for b in range(B):
        dst[b] = src[:, b * W : (b + 1) * W]


def every(i):
    return pl.ds(i, C, stride=L)


def rows(k, n):
    return pl.ds(pl.multiple_of(k * n, 8), n)


class ChannelSum:
    def __init__(self, links, part, landed, own, total, me, ctx):
        self.links, self.part, self.landed, self.own, self.total = links, part, landed, own, total
        self.me, self.peers = me, [(ctx, plus(me, p, 4)) for p in range(1, 4)]

    def scatter(self):
        self.copies = [
            self.links.start(self.part.at[rows(peer[1], 32)], self.landed.at[p], peer)
            for p, peer in enumerate(self.peers)
        ]

    def gather(self):
        arrived(self.copies)
        mine = rows(self.me, 32)
        value = self.part[mine] + self.landed[0] + self.landed[1] + self.landed[2]
        self.own[...] = value
        self.total[mine] = value
        self.copies = [self.links.start(self.own, self.total.at[mine], peer) for peer in self.peers]

    def wait(self):
        arrived(self.copies)


class TileSum:
    def __init__(self, links, place, src, r0, t0, r1, t2, r3, t3, t4, fin):
        self.links, self.place, self.src = links, place, src
        self.r0, self.t0, self.r1, self.t2, self.r3, self.t3, self.t4, self.fin = r0, t0, r1, t2, r3, t3, t4, fin

    def core(self):
        self.copies = [self.links.start(self.src.at[rows(1 - self.place.core, 384)], self.r0, self.place.mate)]

    def scatter(self):
        arrived(self.copies)
        self.t0[...] = self.src[rows(self.place.core, 384)] + self.r0[...]
        self.copies = [
            self.links.start(self.t0.at[rows(k, 24)], self.r1.at[p], dev)
            for p, (k, dev) in enumerate(self.place.plane)
        ]

    def far(self):
        arrived(self.copies)
        v = self.t0[rows(self.place.k, 24)]
        for p in range(15):
            v = v + self.r1[p]
        self.t2[...] = v
        self.copies = [self.links.start(self.t2, self.r3, self.place.far)]

    def gather(self):
        arrived(self.copies)
        v = self.t2[...] + self.r3[...]
        mine = rows(self.place.k, 24)
        self.t3[...] = v
        self.t4[mine] = v
        self.copies = [self.links.start(self.t3, self.t4.at[mine], dev) for _, dev in self.place.plane]

    def join(self):
        arrived(self.copies)
        self.copies = [self.links.start(self.t4, self.fin, self.place.mate)]

    def end(self, write):
        write(self.place.core, self.t4)
        arrived(self.copies)
        write(1 - self.place.core, self.fin)


class Place:
    def __init__(self):
        ctx, me = lax.axis_index("ctx"), lax.axis_index("ch")
        self.ctx, self.me = ctx, me
        self.after, self.before = (plus(ctx, 1, TILES), me), (plus(ctx, TILES - 1, TILES), me)
        self.core, self.y, self.x = lax.rem(ctx, 2), lax.rem(ctx // 2, 4), lax.rem(ctx // 8, 4)
        self.z = ctx // 32
        self.mate = (ctx - self.core + 1 - self.core, me)
        self.far = (lax.rem(ctx + 32, TILES), me)
        self.k = self.x * 4 + self.y
        self.plane = []
        for dx in range(4):
            for dy in range(4):
                if dx or dy:
                    x, y = plus(self.x, dx, 4), plus(self.y, dy, 4)
                    self.plane.append((x * 4 + y, (ctx + (x - self.x) * 8 + (y - self.y) * 2, me)))
        self.k32 = lax.rem(ctx, 32)
        base = ctx - self.k32
        self.half = [(k, (base + k, me)) for k in [plus(self.k32, p, 32) for p in range(1, 32)]]
        self.ch = [(ctx, plus(me, p, 4)) for p in range(1, 4)]

    def everyone(self):
        return [self.after, self.before, self.far] + [dev for _, dev in self.half] + self.ch


class Carries:
    def __init__(self, links, place, d, msg, r1, zs, zr, out, rc):
        self.links, self.place, self.d = links, place, d
        self.msg, self.r1, self.zs, self.zr, self.out, self.rc = msg, r1, zs, zr, out, rc

    def pick(self, up, down):
        sub = lax.broadcasted_iota(jnp.int32, (C, W), 0)
        return jnp.where(sub < 3, up, down) if self.d == 0 else jnp.where(sub < 3, down, up)

    def start(self):
        me = self.place.k32
        self.copies = [self.links.start(self.msg.at[k], self.r1.at[me], dev) for k, dev in self.place.half]
        self.r1[me] = self.msg[me]

    def far(self):
        arrived(self.copies)
        r1 = self.r1
        u = dn = jnp.zeros((C, W), F32)
        for s in range(32):
            u = r1[s, 8:16] * u + r1[s, 0:8]
            dn = r1[31 - s, 8:16] * dn + r1[31 - s, 0:8]
        self.zs[...] = self.pick(u, dn)
        self.copies = [self.links.start(self.zs, self.zr, self.place.far)]

    def back(self):
        arrived(self.copies)
        got, z, r1, out = self.zr[...], self.place.z, self.r1, self.out
        u, dn = jnp.where(z == 1, got, 0.0), jnp.where(z == 0, got, 0.0)
        ups, downs = [], []
        for s in range(32):
            ups.append(u)
            u = r1[s, 8:16] * u + r1[s, 0:8]
            if s < 16:
                out[s] = ups[s]
            downs.append(dn)
            dn = r1[31 - s, 8:16] * dn + r1[31 - s, 0:8]
            if s < 16:
                out[31 - s] = downs[s]
            else:
                out[s] = self.pick(ups[s], out[s])
                out[31 - s] = self.pick(out[31 - s], downs[s])
        me = self.place.k32
        self.copies = [self.links.start(out.at[k], self.rc.at[me], dev) for k, dev in self.place.half]
        self.rc[me] = out[me]

    def wait(self):
        arrived(self.copies)


def block_kernel(
    tok_h, gate_h, cot_h, cw_h, cb_h, sw_h, stw_h, stb_h, dl_h, skip_h,
    out_o, tg_o, gg_o, selg_o, stepg_o,
    tok, gate, cot, cw, cb, sw, stw, stb, dl, skip, in_sem,
    tiles, gates, cots, prev, nxt, prev2, nxt2, send0, send1, ext0, ext1,
    act, sg, part, landed, own, proj, part2, landed2, own2, gp,
    pre, step, drv, g, rt, base, lift, dec, ca, cp, su, sd,
    msg, cr1, czs, czr, cout, crc,
    ss, go, gi, pick, ya, dg, stt, wpad, tgp,
    w_src, w_r0, w_t0, w_r1, w_t2, w_r3, w_t3, w_t4, w_fin,
    send, recv,
):
    pairs = (
        (tok_h, tok), (cw_h, cw), (cb_h, cb), (gate_h, gate), (cot_h, cot), (dl_h, dl),
        (sw_h, sw), (stw_h, stw), (stb_h, stb), (skip_h, skip),
    )
    loads = [pltpu.make_async_copy(a, b, in_sem.at[k]) for k, (a, b) in enumerate(pairs)]
    for load in loads:
        load.start()
    place = Place()
    ctx, me = place.ctx, place.me
    meet = hail(place.everyone())
    meet()
    links = Links(send, recv)
    halo = [
        links.start(tok_h.at[pl.ds(T - 8, 8)], prev, place.after),
        links.start(tok_h.at[pl.ds(0, 8)], nxt, place.before),
    ]
    for load in loads[:3]:
        load.wait()
    by_lanes(tok, tiles)
    for i in range(L):
        for b in range(B):
            ext0[3 + i, :, b * W : (b + 1) * W] = tiles[b, every(i)]

    def conv(d):
        def one(i, carry):
            v = jnp.broadcast_to(cb[d : d + 1], (C, E))
            for k in range(4):
                v = v + cw[d, k : k + 1] * ext0[i + (k if d == 0 else 6 - k)]
            s = sigmoid(v)
            act[d, rows8(i)] = v * s
            sg[d, rows8(i)] = s * (1.0 + v * (1.0 - s))
            return carry

        return one

    lax.fori_loop(3, L, conv(0), 0)
    lax.fori_loop(0, L - 3, conv(1), 0)
    for load in loads[3:]:
        load.wait()
    by_lanes(gate, gates)
    by_lanes(cot, cots)

    def gated(i, carry):
        for b in range(B):
            v = gates[b, every(i)]
            g[rows8(i), b * W : (b + 1) * W] = cots[b, every(i)] * v * sigmoid(v)
        return carry

    lax.fori_loop(0, L, gated, 0, unroll=2)
    for d in range(2):
        ca[d, :, 48:64] = jnp.zeros((32, 16, W), F32)
        cp[d, :, 48:64] = jnp.zeros((32, 16, W), F32)
        for n in range(N):
            rt[d, n] = jnp.broadcast_to(-jnp.exp(dl[d, n : n + 1]) * LOG2E, (C, E))
    lane = lax.broadcasted_iota(jnp.int32, (W, W), 1)
    line = lax.broadcasted_iota(jnp.int32, (W, W), 0)
    for n in range(2 * N):
        at = pl.ds(n * W, W)
        pick[at] = jnp.where(lane == R + n, 1.0, 0.0).astype(jnp.bfloat16)
        lift[0:W, at] = jnp.where(line == R + n, 1.0, 0.0).astype(jnp.bfloat16)
        lift[W : 2 * W, at] = jnp.where(line == R + n, 1.0, 0.0).astype(jnp.bfloat16)
    arrived(halo)
    fill_edges(ext0, prev[5:8], nxt[0:3], ctx > 0, ctx < TILES - 1)
    sums = [ChannelSum(links, part.at[d], landed.at[d], own.at[d], proj.at[d], me, ctx) for d in range(2)]
    lax.fori_loop(0, 3, conv(0), 0)
    part[0] = nn(act[0], sw[0])
    sums[0].scatter()
    lax.fori_loop(L - 3, L, conv(1), 0)
    part[1] = nn(act[1], sw[1])
    sums[1].scatter()
    for d in range(2):
        sums[d].gather()
    def basis(d, i, n):
        return base[d, rows8(i), n * W : (n + 1) * W]

    H = 8
    carries = [Carries(links, place, d, *[r.at[d] for r in (msg, cr1, czs, czr, cout, crc)]) for d in range(2)]
    for d in range(2):
        sums[d].wait()
        spread = jnp.concatenate(parts(proj[d]), axis=1)
        for n in range(0, 2 * N, 2):
            at = pl.ds(n * W, 2 * W)
            base[d, :, at] = jnp.dot(spread, lift[:, at], preferred_element_type=F32)
        pre[d] = nn(proj[d][:, :R], stw[d]) + stb[d : d + 1]

        def prepare(i, carry, d=d):
            st = softplus(pre[d, rows8(i)])
            step[d, rows8(i)] = st
            drv[d, rows8(i)] = st * act[d, rows8(i)]
            return carry

        lax.fori_loop(0, L, prepare, 0, unroll=PREP)
        for half in range(N // H):

            def ends(c, carry, d=d, half=half):
                lanes = pl.ds(pl.multiple_of(c * W, W), W)

                def advance(i, state):
                    f, p, a = state
                    ii = i if d == 0 else L - 1 - i
                    st, dr = step[d, rows8(ii), lanes], drv[d, rows8(ii), lanes]
                    gg = g[rows8(ii), lanes]
                    nf, np_, na = [], [], []
                    for j in range(H):
                        n = half * H + j
                        e = jnp.exp2(st * rt[d, n, :, lanes])
                        dec[d, ii, n, :, lanes] = e
                        nf.append(e * f[j] + basis(d, ii, n) * dr)
                        v = p[j] * e
                        np_.append(v)
                        na.append(a[j] + v * (basis(d, ii, N + n) * gg))
                    return nf, np_, na

                zero = [jnp.zeros((C, W), F32)] * H
                f, p, a = lax.fori_loop(0, L, advance, (zero, [jnp.ones((C, W), F32)] * H, zero), unroll=UNROLL)
                for j in range(H):
                    n = half * H + j
                    slot = n * 2 + c // 3
                    first, second = rows8(lax.rem(c, 3)), rows8(lax.rem(c, 3) + 3)
                    ca[d, slot, first] = f[j]
                    ca[d, slot, second] = a[j]
                    cp[d, slot, first] = p[j]
                    cp[d, slot, second] = p[j]
                return carry

            lax.fori_loop(0, B, ends, 0)

        def totals(q, carry, d=d):
            u = dn = jnp.zeros((C, W), F32)
            pt = jnp.ones((C, W), F32)
            for s in range(C):
                p, back = cp[d, q, pl.ds(s, C, stride=C)], pl.ds(C - 1 - s, C, stride=C)
                u = p * u + ca[d, q, pl.ds(s, C, stride=C)]
                pt = pt * p
                dn = cp[d, q, back] * dn + ca[d, q, back]
            msg[d, q, 0:8] = carries[d].pick(u, dn)
            msg[d, q, 8:16] = pt
            return carry

        lax.fori_loop(0, 32, totals, 0, unroll=4)
        if d == 0:
            carries[0].start()
    carries[0].far()
    carries[0].back()
    carries[1].start()
    carries[0].wait()

    Q = 3
    QW = Q * W

    def folded(v):
        r = v[:, :W]
        for k in range(1, Q):
            r = r + v[:, k * W : (k + 1) * W]
        return r

    def wide(v):
        return jnp.concatenate([v] * Q, axis=1)

    def begin(src, first, half, cb, j):
        n = half * H + j
        return jnp.concatenate([src[n * 2 + cb, pl.ds((first + k) * 8, 8)] for k in range(Q)], axis=1)

    blocks = [(half, cb) for half in range(N // H) for cb in range(B // Q)]

    def sweep(d, between):
        def starts(q, carry):
            u = dn = crc[d, q]
            for s in range(C):
                at, back = pl.ds(s, C, stride=C), pl.ds(C - 1 - s, C, stride=C)
                su[q, at] = u
                u = cp[d, q, at] * u + ca[d, q, at]
                sd[q, back] = dn
                dn = cp[d, q, back] * dn + ca[d, q, back]
            return carry

        lax.fori_loop(0, 32, starts, 0, unroll=4)
        fs, bs = (su, sd) if d == 0 else (sd, su)
        for half, cb in blocks:
            for step_on in between.get((half, cb), ()):
                step_on()
            lanes = pl.ds(cb * QW, QW)

            def forward(i, state, half=half, cb=cb, lanes=lanes):
                ii = i if d == 0 else L - 1 - i
                dr, gg = drv[d, rows8(ii), lanes], g[rows8(ii), lanes]
                if half == 0:
                    y = skip[d : d + 1, lanes] * act[d, rows8(ii), lanes]
                    if d == 1:
                        y = y + ya[rows8(ii), lanes]
                else:
                    y = ya[rows8(ii), lanes]
                new = []
                for j in range(H):
                    n = half * H + j
                    s = dec[d, ii, n, :, lanes] * state[j] + wide(basis(d, ii, n)) * dr
                    y = y + wide(basis(d, ii, N + n)) * s
                    v, at = folded(s * gg), pl.ds(n * W, W)
                    go[rows8(ii), at] = v if cb == 0 else go[rows8(ii), at] + v
                    ss[i + 1, j] = s
                    new.append(s)
                ya[rows8(ii), lanes] = y
                return new

            first = [begin(fs, 0, half, cb, j) for j in range(H)]
            for j in range(H):
                ss[0, j] = first[j]
            lax.fori_loop(0, L, forward, first, unroll=SW)

            def retreat(t, carried, half=half, cb=cb, lanes=lanes):
                i = L - 1 - t
                ii = i if d == 0 else L - 1 - i
                dr, gg = drv[d, rows8(ii), lanes], g[rows8(ii), lanes]
                if half == 0:
                    a1 = a2 = jnp.zeros((C, QW), F32)
                else:
                    a1, a2 = stt[rows8(ii), lanes], dg[rows8(ii), lanes]
                new = []
                for j in range(H):
                    n = half * H + j
                    adj = carried[j] + wide(basis(d, ii, N + n)) * gg
                    back = dec[d, ii, n, :, lanes] * adj
                    a1 = a1 + (back * ss[i, j]) * rt[d, n, :, lanes]
                    a2 = a2 + adj * wide(basis(d, ii, n))
                    v, at = folded(adj * dr), pl.ds(n * W, W)
                    gi[rows8(ii), at] = v if cb == 0 else gi[rows8(ii), at] + v
                    new.append(back)
                stt[rows8(ii), lanes] = a1
                dg[rows8(ii), lanes] = a2
                return new

            lax.fori_loop(0, L, retreat, [begin(bs, 3, half, cb, j) for j in range(H)], unroll=SW)

        for step_on in between["close"]:
            step_on()

        def close(i, carry):
            at = rows8(i)
            slope = dg[at]
            ga = g[at] * skip[d : d + 1] + slope * step[d, at]
            stt[at] = (stt[at] * LN2 + slope * act[d, at]) * sigmoid(pre[d, at])
            drv[d, at] = ga
            return carry

        lax.fori_loop(0, L, close, 0)
        wpad[0:R] = stw[d]
        part2[d] = nt(stt[...], wpad[...])

        total = part2[d]
        for k in range(0, 2 * N, 4):
            source = (gi if k < N else go)[:, (k % N) * W : (k % N + 4) * W]
            for half in parts(source):
                total = total + jnp.dot(half, pick[k * W : (k + 4) * W], preferred_element_type=F32)
        part2[d] = total

    wpad[...] = jnp.zeros_like(wpad)
    back_sums = [ChannelSum(links, part2.at[d], landed2.at[d], own2.at[d], gp.at[d], me, ctx) for d in range(2)]
    weights = [
        TileSum(links, place, *[r.at[k] for r in (w_src, w_r0, w_t0, w_r1, w_t2, w_r3, w_t3, w_t4, w_fin)])
        for k in range(4)
    ]
    s0, s1, t0, t1 = weights

    def step_part(d, stream):
        v = tn(proj[d], stt[...])
        for b in range(B):
            stream.src[b * W : (b + 1) * W] = v[:, b * W : (b + 1) * W]

    def select_part(d, stream, ext):
        stream.src[...] = tn(act[d], gp[d])
        stream.core()
        tgp[...] = nt(gp[d], sw[d])

        def conv_grad(i, carry):
            ext[3 + i] = (drv[d, rows8(i)] + tgp[rows8(i)]) * sg[d, rows8(i)]
            return carry

        lax.fori_loop(0, L, conv_grad, 0)

    def step_end(d):
        def write(core, src):
            for b in range(3):
                lanes = pl.ds(pl.multiple_of(core * 384 + b * W, W), W)
                stepg_o[d, :, lanes] = src[b * W : b * W + R]

        return write

    def select_end(d):
        def write(core, src):
            selg_o[d, rows(core, 384)] = src[...]

        return write

    sweep(0, {(0, 1): [carries[1].far], "close": [carries[1].back]})
    back_sums[0].scatter()
    step_part(0, s0)
    s0.core()
    carries[1].wait()
    sweep(1, {(0, 1): [back_sums[0].gather, s0.scatter], "close": [s0.far]})
    back_sums[1].scatter()
    step_part(1, s1)
    s1.core()
    back_sums[0].wait()
    select_part(0, t0, ext0)
    back_sums[1].gather()
    s0.gather()
    s1.scatter()
    t0.scatter()

    def gates_back(i, carry):
        for b in range(B):
            v, ct, y = gates[b, every(i)], cots[b, every(i)], ya[rows8(i), b * W : (b + 1) * W]
            s = sigmoid(v)
            gates[b, every(i)] = y * v * s
            cots[b, every(i)] = ct * y * (s * (1.0 + v * (1.0 - s)))
        return carry

    lax.fori_loop(0, L, gates_back, 0, unroll=2)
    for b in range(B):
        out_o[:, b * W : (b + 1) * W] = gates[b]
        gg_o[:, b * W : (b + 1) * W] = cots[b]
    back_sums[1].wait()
    select_part(1, t1, ext1)
    for k in range(3):
        send0[k : k + 1] = ext0[3 + k, 0:1]
        send1[k : k + 1] = ext1[3 + L - 3 + k, C - 1 : C]
    halo = [links.start(send0, nxt2, place.before), links.start(send1, prev2, place.after)]
    t1.scatter()
    s1.far()
    t0.far()
    s0.join()

    t1.far()
    s1.gather()
    t0.gather()
    arrived(halo)
    fill_edges(ext0, prev2[0:3], nxt2[0:3], ctx > 0, ctx < TILES - 1)
    fill_edges(ext1, prev2[0:3], nxt2[0:3], ctx > 0, ctx < TILES - 1)

    def conv_back(i, carry):
        v = jnp.zeros((C, E), F32)
        for k in range(4):
            v = v + cw[0, k : k + 1] * ext0[i + 6 - k] + cw[1, k : k + 1] * ext1[i + k]
        for b in range(B):
            tiles[b, every(i)] = v[:, b * W : (b + 1) * W]
        return carry

    lax.fori_loop(0, L, conv_back, 0)
    for b in range(B):
        tg_o[:, b * W : (b + 1) * W] = tiles[b]
    t1.gather()
    s1.join()
    t0.join()
    s0.end(step_end(0))
    t1.join()
    s1.end(step_end(1))
    t0.end(select_end(0))
    t1.end(select_end(1))
    links.finish()


UNROLL = 4
PREP = 2
SW = 2
LIMIT = 49 << 20


def store_kernel(*refs):
    ins, outs, sem = refs[:5], refs[5:10], refs[10]
    copies = [pltpu.make_async_copy(a, b, sem.at[k]) for k, (a, b) in enumerate(zip(ins, outs))]
    for copy in copies:
        copy.start()
    for copy in copies:
        copy.wait()


def on_device(*args):
    v = lambda *shape: pltpu.VMEM(shape, F32)
    copies = 2 + 12 + 2 * 63 + 12 + 2 + 4 * 33
    hbm = pl.BlockSpec(memory_space=pltpu.HBM)
    shapes = (sds(T, E), sds(T, E), sds(T, E), sds(2, E, W), sds(2, R, E))
    args = [pltpu.with_memory_space_constraint(a, pltpu.HBM) for a in args]
    results = pl.pallas_call(
        block_kernel,
        out_shape=shapes,
        in_specs=[hbm] * 10,
        out_specs=(VM,) * 5,
        scratch_shapes=[
            v(T, E), v(T, E), v(T, E), v(2, 4, E), v(2, E), v(2, E, W), v(2, R, E), v(2, E), v(2, N, E), v(2, E),
            pltpu.SemaphoreType.DMA((10,)),
            v(B, T, W), v(B, T, W), v(B, T, W), v(8, E), v(8, E), v(8, E), v(8, E), v(8, E), v(8, E),
            v(L + 6, C, E), v(L + 6, C, E),
            v(2, T, E), v(2, T, E), v(2, T, W), v(2, 3, 32, W), v(2, 32, W), v(2, T, W),
            v(2, T, W), v(2, 3, 32, W), v(2, 32, W), v(2, T, W),
            v(2, T, E), v(2, T, E), v(2, T, E), v(T, E), v(2, N, C, E), v(2, T, 2 * N * W),
            pltpu.VMEM((2 * W, 2 * N * W), jnp.bfloat16),
            v(2, L, N, C, E), v(2, 32, 64, W), v(2, 32, 64, W), v(32, 64, W), v(32, 64, W),
            v(2, 32, 16, W), v(2, 32, 16, W), v(2, C, W), v(2, C, W), v(2, 32, C, W), v(2, 32, C, W),
            v(L + 1, 8, C, 3 * W), v(T, N * W), v(T, N * W), pltpu.VMEM((2 * N * W, W), jnp.bfloat16), v(T, E), v(T, E), v(T, E), v(W, E), v(T, E),
            v(4, E, W), v(4, 384, W), v(4, 384, W), v(4, 15, 24, W), v(4, 24, W), v(4, 24, W), v(4, 24, W),
            v(4, 384, W), v(4, 384, W),
            pltpu.SemaphoreType.DMA((copies,)),
            pltpu.SemaphoreType.DMA((copies,)),
        ],
        compiler_params=pltpu.CompilerParams(
            collective_id=0, has_side_effects=True, vmem_limit_bytes=LIMIT
        ),
        name="block",
    )(*args)
    return pl.pallas_call(
        store_kernel,
        out_shape=shapes,
        in_specs=[VM] * 5,
        out_specs=(hbm,) * 5,
        scratch_shapes=[pltpu.SemaphoreType.DMA((5,))],
        compiler_params=pltpu.CompilerParams(vmem_limit_bytes=1 << 20),
        name="store",
    )(*results)


def solution(mesh):
    row = P("ctx", "ch")
    in_specs = (
        row,
        row,
        row,
        P(None, None, "ch"),
        P(None, "ch"),
        P(None, "ch", None),
        P(None, None, "ch"),
        P(None, "ch"),
        P(None, None, "ch"),
        P(None, "ch"),
    )
    out_specs = (row, row, row, P(None, "ch", None), P(None, None, "ch"))
    return jax.shard_map(on_device, mesh=mesh, in_specs=in_specs, out_specs=out_specs, check_vma=False)
```

```python
import jax
import jax.numpy as jnp
from jax import lax
from jax.experimental import pallas as pl
from jax.experimental.pallas import tpu as pltpu
from jax.sharding import PartitionSpec as P

F32 = jnp.float32
MESH = pl.DeviceIdType.MESH

T = 128
C = 8
L = 16
E = 768
N = 16
R = 96
W = 128
B = E // W
TILES = 64

VM = pl.BlockSpec(memory_space=pltpu.VMEM)


def sds(*shape):
    return jax.ShapeDtypeStruct(shape, F32)


LOG2E = 1.4426950408889634
LN2 = 0.6931471805599453


def sigmoid(v):
    return 1.0 / (1.0 + jnp.exp(-v))


def softplus(v):
    return jnp.maximum(v, 0.0) + jnp.log1p(jnp.exp(-jnp.abs(v)))


def rows8(i):
    return pl.ds(pl.multiple_of(i * 8, 8), 8)


def parts(a):
    high = a.astype(jnp.bfloat16)
    return high, (a - high.astype(F32)).astype(jnp.bfloat16)


def product(a, b, left, right):
    (ah, al), (bh, bl) = parts(a), parts(b)

    def dot(u, v):
        return lax.dot_general(u, v, (((left,), (right,)), ((), ())), preferred_element_type=F32)

    return dot(ah, bh) + (dot(ah, bl) + dot(al, bh))


def nn(a, b):
    return product(a, b, 1, 0)


def nt(a, b):
    return product(a, b, 1, 1)


def tn(a, b):
    return product(a, b, 0, 0)


class Links:
    def __init__(self, send, recv):
        self.send, self.recv, self.used = send, recv, 0
        self.all = []

    def start(self, src, dst, device):
        k = self.used
        self.used += 1
        copy = pltpu.make_async_remote_copy(
            src_ref=src,
            dst_ref=dst,
            send_sem=self.send.at[k],
            recv_sem=self.recv.at[k],
            device_id=device,
            device_id_type=MESH,
        )
        copy.start()
        self.all.append(copy)
        return copy

    def finish(self):
        for copy in self.all:
            copy.wait_send()


def arrived(copies):
    for copy in copies:
        copy.wait_recv()


def hail(devices):
    barrier = pltpu.get_barrier_semaphore()
    for device in devices:
        pl.semaphore_signal(barrier, inc=1, device_id=device, device_id_type=MESH)
    return lambda: pl.semaphore_wait(barrier, len(devices))


def plus(a, p, n):
    return lax.rem(a + p, n)


def fill_edges(ext, prev, nxt, has_prev, has_next):
    sub = lax.broadcasted_iota(jnp.int32, (C, E), 0)
    for k in range(3):
        last = ext[3 + L - 3 + k]
        row = jnp.broadcast_to(prev[k : k + 1], (C, E))
        row = jnp.where(has_prev, row, 0.0)
        ext[k] = jnp.where(sub == 0, row, pltpu.roll(last, 1, 0))
        first = ext[3 + k]
        row = jnp.broadcast_to(nxt[k : k + 1], (C, E))
        row = jnp.where(has_next, row, 0.0)
        ext[3 + L + k] = jnp.where(sub == C - 1, row, pltpu.roll(first, C - 1, 0))


def by_lanes(src, dst):
    for b in range(B):
        dst[b] = src[:, b * W : (b + 1) * W]


def every(i):
    return pl.ds(i, C, stride=L)


def rows(k, n):
    return pl.ds(pl.multiple_of(k * n, 8), n)


class ChannelSum:
    def __init__(self, links, part, landed, own, total, me, ctx):
        self.links, self.part, self.landed, self.own, self.total = links, part, landed, own, total
        self.me, self.peers = me, [(ctx, plus(me, p, 4)) for p in range(1, 4)]

    def scatter(self):
        self.copies = [
            self.links.start(self.part.at[rows(peer[1], 32)], self.landed.at[p], peer)
            for p, peer in enumerate(self.peers)
        ]

    def gather(self):
        arrived(self.copies)
        mine = rows(self.me, 32)
        value = self.part[mine] + self.landed[0] + self.landed[1] + self.landed[2]
        self.own[...] = value
        self.total[mine] = value
        self.copies = [self.links.start(self.own, self.total.at[mine], peer) for peer in self.peers]

    def wait(self):
        arrived(self.copies)


class TileSum:
    def __init__(self, links, place, src, r0, t0, r1, t2, r3, t3, t4, fin):
        self.links, self.place, self.src = links, place, src
        self.r0, self.t0, self.r1, self.t2, self.r3, self.t3, self.t4, self.fin = r0, t0, r1, t2, r3, t3, t4, fin

    def core(self):
        self.copies = [self.links.start(self.src.at[rows(1 - self.place.core, 384)], self.r0, self.place.mate)]

    def scatter(self):
        arrived(self.copies)
        self.t0[...] = self.src[rows(self.place.core, 384)] + self.r0[...]
        self.copies = [
            self.links.start(self.t0.at[rows(k, 24)], self.r1.at[p], dev)
            for p, (k, dev) in enumerate(self.place.plane)
        ]

    def far(self):
        arrived(self.copies)
        v = self.t0[rows(self.place.k, 24)]
        for p in range(15):
            v = v + self.r1[p]
        self.t2[...] = v
        self.copies = [self.links.start(self.t2, self.r3, self.place.far)]

    def gather(self):
        arrived(self.copies)
        v = self.t2[...] + self.r3[...]
        mine = rows(self.place.k, 24)
        self.t3[...] = v
        self.t4[mine] = v
        self.copies = [self.links.start(self.t3, self.t4.at[mine], dev) for _, dev in self.place.plane]

    def join(self):
        arrived(self.copies)
        self.copies = [self.links.start(self.t4, self.fin, self.place.mate)]

    def end(self, write):
        write(self.place.core, self.t4)
        arrived(self.copies)
        write(1 - self.place.core, self.fin)


class Place:
    def __init__(self):
        ctx, me = lax.axis_index("ctx"), lax.axis_index("ch")
        self.ctx, self.me = ctx, me
        self.after, self.before = (plus(ctx, 1, TILES), me), (plus(ctx, TILES - 1, TILES), me)
        self.core, self.y, self.x = lax.rem(ctx, 2), lax.rem(ctx // 2, 4), lax.rem(ctx // 8, 4)
        self.z = ctx // 32
        self.mate = (ctx - self.core + 1 - self.core, me)
        self.far = (lax.rem(ctx + 32, TILES), me)
        self.k = self.x * 4 + self.y
        self.plane = []
        for dx in range(4):
            for dy in range(4):
                if dx or dy:
                    x, y = plus(self.x, dx, 4), plus(self.y, dy, 4)
                    self.plane.append((x * 4 + y, (ctx + (x - self.x) * 8 + (y - self.y) * 2, me)))
        self.k32 = lax.rem(ctx, 32)
        base = ctx - self.k32
        self.half = [(k, (base + k, me)) for k in [plus(self.k32, p, 32) for p in range(1, 32)]]
        self.ch = [(ctx, plus(me, p, 4)) for p in range(1, 4)]

    def everyone(self):
        return [self.after, self.before, self.far] + [dev for _, dev in self.half] + self.ch


class Carries:
    def __init__(self, links, place, d, msg, r1, zs, zr, out, rc):
        self.links, self.place, self.d = links, place, d
        self.msg, self.r1, self.zs, self.zr, self.out, self.rc = msg, r1, zs, zr, out, rc

    def pick(self, up, down):
        sub = lax.broadcasted_iota(jnp.int32, (C, W), 0)
        return jnp.where(sub < 3, up, down) if self.d == 0 else jnp.where(sub < 3, down, up)

    def start(self):
        me = self.place.k32
        self.copies = [self.links.start(self.msg.at[k], self.r1.at[me], dev) for k, dev in self.place.half]
        self.r1[me] = self.msg[me]

    def far(self):
        arrived(self.copies)
        r1 = self.r1
        u = dn = jnp.zeros((C, W), F32)
        for s in range(32):
            u = r1[s, 8:16] * u + r1[s, 0:8]
            dn = r1[31 - s, 8:16] * dn + r1[31 - s, 0:8]
        self.zs[...] = self.pick(u, dn)
        self.copies = [self.links.start(self.zs, self.zr, self.place.far)]

    def back(self):
        arrived(self.copies)
        got, z, r1, out = self.zr[...], self.place.z, self.r1, self.out
        u, dn = jnp.where(z == 1, got, 0.0), jnp.where(z == 0, got, 0.0)
        ups, downs = [], []
        for s in range(32):
            ups.append(u)
            u = r1[s, 8:16] * u + r1[s, 0:8]
            if s < 16:
                out[s] = ups[s]
            downs.append(dn)
            dn = r1[31 - s, 8:16] * dn + r1[31 - s, 0:8]
            if s < 16:
                out[31 - s] = downs[s]
            else:
                out[s] = self.pick(ups[s], out[s])
                out[31 - s] = self.pick(out[31 - s], downs[s])
        me = self.place.k32
        self.copies = [self.links.start(out.at[k], self.rc.at[me], dev) for k, dev in self.place.half]
        self.rc[me] = out[me]

    def wait(self):
        arrived(self.copies)


def block_kernel(
    tok_h, gate_h, cot_h, cw_h, cb_h, sw_h, stw_h, stb_h, dl_h, skip_h,
    out_o, tg_o, gg_o, selg_o, stepg_o,
    tok, gate, cot, cw, cb, sw, stw, stb, dl, skip, in_sem,
    tiles, gates, cots, prev, nxt, prev2, nxt2, send0, send1, ext0, ext1,
    act, sg, part, landed, own, proj, part2, landed2, own2, gp,
    pre, step, drv, g, rt, base, lift, dec, ca, cp, su, sd,
    msg, cr1, czs, czr, cout, crc,
    ss, go, gi, pick, ya, dg, stt, wpad, tgp,
    w_src, w_r0, w_t0, w_r1, w_t2, w_r3, w_t3, w_t4, w_fin,
    send, recv,
):
    pairs = (
        (tok_h, tok), (cw_h, cw), (cb_h, cb), (gate_h, gate), (cot_h, cot), (dl_h, dl),
        (sw_h, sw), (stw_h, stw), (stb_h, stb), (skip_h, skip),
    )
    loads = [pltpu.make_async_copy(a, b, in_sem.at[k]) for k, (a, b) in enumerate(pairs)]
    for load in loads:
        load.start()
    place = Place()
    ctx, me = place.ctx, place.me
    meet = hail(place.everyone())
    meet()
    links = Links(send, recv)
    halo = [
        links.start(tok_h.at[pl.ds(T - 8, 8)], prev, place.after),
        links.start(tok_h.at[pl.ds(0, 8)], nxt, place.before),
    ]
    for load in loads[:3]:
        load.wait()
    by_lanes(tok, tiles)
    for i in range(L):
        for b in range(B):
            ext0[3 + i, :, b * W : (b + 1) * W] = tiles[b, every(i)]

    def conv(d):
        def one(i, carry):
            v = jnp.broadcast_to(cb[d : d + 1], (C, E))
            for k in range(4):
                v = v + cw[d, k : k + 1] * ext0[i + (k if d == 0 else 6 - k)]
            s = sigmoid(v)
            act[d, rows8(i)] = v * s
            sg[d, rows8(i)] = s * (1.0 + v * (1.0 - s))
            return carry

        return one

    lax.fori_loop(3, L, conv(0), 0)
    lax.fori_loop(0, L - 3, conv(1), 0)
    for load in loads[3:]:
        load.wait()
    by_lanes(gate, gates)
    by_lanes(cot, cots)

    def gated(i, carry):
        for b in range(B):
            v = gates[b, every(i)]
            g[rows8(i), b * W : (b + 1) * W] = cots[b, every(i)] * v * sigmoid(v)
        return carry

    lax.fori_loop(0, L, gated, 0, unroll=2)
    for d in range(2):
        ca[d, :, 48:64] = jnp.zeros((32, 16, W), F32)
        cp[d, :, 48:64] = jnp.zeros((32, 16, W), F32)
        for n in range(N):
            rt[d, n] = jnp.broadcast_to(-jnp.exp(dl[d, n : n + 1]) * LOG2E, (C, E))
    lane = lax.broadcasted_iota(jnp.int32, (W, W), 1)
    line = lax.broadcasted_iota(jnp.int32, (W, W), 0)
    for n in range(2 * N):
        at = pl.ds(n * W, W)
        pick[at] = jnp.where(lane == R + n, 1.0, 0.0).astype(jnp.bfloat16)
        lift[0:W, at] = jnp.where(line == R + n, 1.0, 0.0).astype(jnp.bfloat16)
        lift[W : 2 * W, at] = jnp.where(line == R + n, 1.0, 0.0).astype(jnp.bfloat16)
    arrived(halo)
    fill_edges(ext0, prev[5:8], nxt[0:3], ctx > 0, ctx < TILES - 1)
    sums = [ChannelSum(links, part.at[d], landed.at[d], own.at[d], proj.at[d], me, ctx) for d in range(2)]
    lax.fori_loop(0, 3, conv(0), 0)
    part[0] = nn(act[0], sw[0])
    sums[0].scatter()
    lax.fori_loop(L - 3, L, conv(1), 0)
    part[1] = nn(act[1], sw[1])
    sums[1].scatter()
    for d in range(2):
        sums[d].gather()
    def basis(d, i, n):
        return base[d, rows8(i), n * W : (n + 1) * W]

    H = 8
    carries = [Carries(links, place, d, *[r.at[d] for r in (msg, cr1, czs, czr, cout, crc)]) for d in range(2)]
    for d in range(2):
        sums[d].wait()
        spread = jnp.concatenate(parts(proj[d]), axis=1)
        for n in range(0, 2 * N, 2):
            at = pl.ds(n * W, 2 * W)
            base[d, :, at] = jnp.dot(spread, lift[:, at], preferred_element_type=F32)
        pre[d] = nn(proj[d][:, :R], stw[d]) + stb[d : d + 1]

        def prepare(i, carry, d=d):
            st = softplus(pre[d, rows8(i)])
            step[d, rows8(i)] = st
            drv[d, rows8(i)] = st * act[d, rows8(i)]
            return carry

        lax.fori_loop(0, L, prepare, 0, unroll=PREP)
        for half in range(N // H):

            def ends(c, carry, d=d, half=half):
                lanes = pl.ds(pl.multiple_of(c * W, W), W)

                def advance(i, state):
                    f, p, a = state
                    ii = i if d == 0 else L - 1 - i
                    st, dr = step[d, rows8(ii), lanes], drv[d, rows8(ii), lanes]
                    gg = g[rows8(ii), lanes]
                    nf, np_, na = [], [], []
                    for j in range(H):
                        n = half * H + j
                        e = jnp.exp2(st * rt[d, n, :, lanes])
                        dec[d, ii, n, :, lanes] = e
                        nf.append(e * f[j] + basis(d, ii, n) * dr)
                        v = p[j] * e
                        np_.append(v)
                        na.append(a[j] + v * (basis(d, ii, N + n) * gg))
                    return nf, np_, na

                zero = [jnp.zeros((C, W), F32)] * H
                f, p, a = lax.fori_loop(0, L, advance, (zero, [jnp.ones((C, W), F32)] * H, zero), unroll=UNROLL[d])
                for j in range(H):
                    n = half * H + j
                    slot = n * 2 + c // 3
                    first, second = rows8(lax.rem(c, 3)), rows8(lax.rem(c, 3) + 3)
                    ca[d, slot, first] = f[j]
                    ca[d, slot, second] = a[j]
                    cp[d, slot, first] = p[j]
                    cp[d, slot, second] = p[j]
                return carry

            lax.fori_loop(0, B, ends, 0)

        def totals(q, carry, d=d):
            u = dn = jnp.zeros((C, W), F32)
            pt = jnp.ones((C, W), F32)
            for s in range(C):
                p, back = cp[d, q, pl.ds(s, C, stride=C)], pl.ds(C - 1 - s, C, stride=C)
                u = p * u + ca[d, q, pl.ds(s, C, stride=C)]
                pt = pt * p
                dn = cp[d, q, back] * dn + ca[d, q, back]
            msg[d, q, 0:8] = carries[d].pick(u, dn)
            msg[d, q, 8:16] = pt
            return carry

        lax.fori_loop(0, 32, totals, 0, unroll=4)
        if d == 0:
            carries[0].start()
    carries[1].start()
    carries[0].far()
    carries[0].back()
    carries[1].far()
    carries[0].wait()
    carries[1].back()

    Q = 3
    QW = Q * W

    def folded(v):
        r = v[:, :W]
        for k in range(1, Q):
            r = r + v[:, k * W : (k + 1) * W]
        return r

    def wide(v):
        return jnp.concatenate([v] * Q, axis=1)

    def begin(src, first, half, cb, j):
        n = half * H + j
        return jnp.concatenate([src[n * 2 + cb, pl.ds((first + k) * 8, 8)] for k in range(Q)], axis=1)

    blocks = [(half, cb) for half in range(N // H) for cb in range(B // Q)]

    def sweep(d, between):
        def starts(q, carry):
            u = dn = crc[d, q]
            for s in range(C):
                at, back = pl.ds(s, C, stride=C), pl.ds(C - 1 - s, C, stride=C)
                su[q, at] = u
                u = cp[d, q, at] * u + ca[d, q, at]
                sd[q, back] = dn
                dn = cp[d, q, back] * dn + ca[d, q, back]
            return carry

        lax.fori_loop(0, 32, starts, 0, unroll=4)
        fs, bs = (su, sd) if d == 0 else (sd, su)
        for half, cb in blocks:
            for step_on in between.get((half, cb), ()):
                step_on()
            lanes = pl.ds(cb * QW, QW)

            def forward(i, state, half=half, cb=cb, lanes=lanes):
                ii = i if d == 0 else L - 1 - i
                dr, gg = drv[d, rows8(ii), lanes], g[rows8(ii), lanes]
                if half == 0:
                    y = skip[d : d + 1, lanes] * act[d, rows8(ii), lanes]
                    if d == 1:
                        y = y + ya[rows8(ii), lanes]
                else:
                    y = ya[rows8(ii), lanes]
                new = []
                for j in range(H):
                    n = half * H + j
                    s = dec[d, ii, n, :, lanes] * state[j] + wide(basis(d, ii, n)) * dr
                    y = y + wide(basis(d, ii, N + n)) * s
                    v, at = folded(s * gg), pl.ds(n * W, W)
                    go[rows8(ii), at] = v if cb == 0 else go[rows8(ii), at] + v
                    ss[i + 1, j] = s
                    new.append(s)
                ya[rows8(ii), lanes] = y
                return new

            first = [begin(fs, 0, half, cb, j) for j in range(H)]
            for j in range(H):
                ss[0, j] = first[j]
            lax.fori_loop(0, L, forward, first, unroll=SW)

            def retreat(t, carried, half=half, cb=cb, lanes=lanes):
                i = L - 1 - t
                ii = i if d == 0 else L - 1 - i
                dr, gg = drv[d, rows8(ii), lanes], g[rows8(ii), lanes]
                if half == 0:
                    a1 = a2 = jnp.zeros((C, QW), F32)
                else:
                    a1, a2 = stt[rows8(ii), lanes], dg[rows8(ii), lanes]
                new = []
                for j in range(H):
                    n = half * H + j
                    adj = carried[j] + wide(basis(d, ii, N + n)) * gg
                    back = dec[d, ii, n, :, lanes] * adj
                    a1 = a1 + (back * ss[i, j]) * rt[d, n, :, lanes]
                    a2 = a2 + adj * wide(basis(d, ii, n))
                    v, at = folded(adj * dr), pl.ds(n * W, W)
                    gi[rows8(ii), at] = v if cb == 0 else gi[rows8(ii), at] + v
                    new.append(back)
                stt[rows8(ii), lanes] = a1
                dg[rows8(ii), lanes] = a2
                return new

            lax.fori_loop(0, L, retreat, [begin(bs, 3, half, cb, j) for j in range(H)], unroll=SW)

        def close(i, carry):
            at = rows8(i)
            slope = dg[at]
            ga = g[at] * skip[d : d + 1] + slope * step[d, at]
            stt[at] = (stt[at] * LN2 + slope * act[d, at]) * sigmoid(pre[d, at])
            drv[d, at] = ga
            return carry

        lax.fori_loop(0, L, close, 0)
        wpad[0:R] = stw[d]
        part2[d] = nt(stt[...], wpad[...])

        total = part2[d]
        for k in range(0, 2 * N, 4):
            source = (gi if k < N else go)[:, (k % N) * W : (k % N + 4) * W]
            for half in parts(source):
                total = total + jnp.dot(half, pick[k * W : (k + 4) * W], preferred_element_type=F32)
        part2[d] = total

    wpad[...] = jnp.zeros_like(wpad)
    back_sums = [ChannelSum(links, part2.at[d], landed2.at[d], own2.at[d], gp.at[d], me, ctx) for d in range(2)]
    weights = [
        TileSum(links, place, *[r.at[k] for r in (w_src, w_r0, w_t0, w_r1, w_t2, w_r3, w_t3, w_t4, w_fin)])
        for k in range(4)
    ]
    s0, s1, t0, t1 = weights

    def step_part(d, stream):
        v = tn(proj[d], stt[...])
        for b in range(B):
            stream.src[b * W : (b + 1) * W] = v[:, b * W : (b + 1) * W]

    def select_part(d, stream, ext):
        stream.src[...] = tn(act[d], gp[d])
        stream.core()
        tgp[...] = nt(gp[d], sw[d])

        def conv_grad(i, carry):
            ext[3 + i] = (drv[d, rows8(i)] + tgp[rows8(i)]) * sg[d, rows8(i)]
            return carry

        lax.fori_loop(0, L, conv_grad, 0)

    def step_end(d):
        def write(core, src):
            for b in range(3):
                lanes = pl.ds(pl.multiple_of(core * 384 + b * W, W), W)
                stepg_o[d, :, lanes] = src[b * W : b * W + R]

        return write

    def select_end(d):
        def write(core, src):
            selg_o[d, rows(core, 384)] = src[...]

        return write

    sweep(0, {})
    back_sums[0].scatter()
    step_part(0, s0)
    s0.core()
    carries[1].wait()
    sweep(1, {(0, 1): [back_sums[0].gather, s0.scatter]})
    back_sums[1].scatter()
    step_part(1, s1)
    s1.core()
    back_sums[0].wait()
    select_part(0, t0, ext0)
    s0.far()
    back_sums[1].gather()
    s0.gather()
    s1.scatter()
    t0.scatter()

    def gates_back(i, carry):
        for b in range(B):
            v, ct, y = gates[b, every(i)], cots[b, every(i)], ya[rows8(i), b * W : (b + 1) * W]
            s = sigmoid(v)
            gates[b, every(i)] = y * v * s
            cots[b, every(i)] = ct * y * (s * (1.0 + v * (1.0 - s)))
        return carry

    lax.fori_loop(0, L, gates_back, 0, unroll=2)
    for b in range(B):
        out_o[:, b * W : (b + 1) * W] = gates[b]
        gg_o[:, b * W : (b + 1) * W] = cots[b]
    back_sums[1].wait()
    select_part(1, t1, ext1)
    for k in range(3):
        send0[k : k + 1] = ext0[3 + k, 0:1]
        send1[k : k + 1] = ext1[3 + L - 3 + k, C - 1 : C]
    halo = [links.start(send0, nxt2, place.before), links.start(send1, prev2, place.after)]
    t1.scatter()
    s1.far()
    t0.far()
    s0.join()

    t1.far()
    s1.gather()
    t0.gather()
    arrived(halo)
    fill_edges(ext0, prev2[0:3], nxt2[0:3], ctx > 0, ctx < TILES - 1)
    fill_edges(ext1, prev2[0:3], nxt2[0:3], ctx > 0, ctx < TILES - 1)

    def conv_back(i, carry):
        v = jnp.zeros((C, E), F32)
        for k in range(4):
            v = v + cw[0, k : k + 1] * ext0[i + 6 - k] + cw[1, k : k + 1] * ext1[i + k]
        for b in range(B):
            tiles[b, every(i)] = v[:, b * W : (b + 1) * W]
        return carry

    lax.fori_loop(0, L, conv_back, 0)
    for b in range(B):
        tg_o[:, b * W : (b + 1) * W] = tiles[b]
    t1.gather()
    s1.join()
    t0.join()
    s0.end(step_end(0))
    t1.join()
    s1.end(step_end(1))
    t0.end(select_end(0))
    t1.end(select_end(1))
    links.finish()


UNROLL = (8, 4)
PREP = 2
SW = 2
LIMIT = 49 << 20


def store_kernel(*refs):
    ins, outs, sem = refs[:5], refs[5:10], refs[10]
    copies = [pltpu.make_async_copy(a, b, sem.at[k]) for k, (a, b) in enumerate(zip(ins, outs))]
    for copy in copies:
        copy.start()
    for copy in copies:
        copy.wait()


def on_device(*args):
    v = lambda *shape: pltpu.VMEM(shape, F32)
    copies = 2 + 12 + 2 * 63 + 12 + 2 + 4 * 33
    hbm = pl.BlockSpec(memory_space=pltpu.HBM)
    shapes = (sds(T, E), sds(T, E), sds(T, E), sds(2, E, W), sds(2, R, E))
    args = [pltpu.with_memory_space_constraint(a, pltpu.HBM) for a in args]
    results = pl.pallas_call(
        block_kernel,
        out_shape=shapes,
        in_specs=[hbm] * 10,
        out_specs=(VM,) * 5,
        scratch_shapes=[
            v(T, E), v(T, E), v(T, E), v(2, 4, E), v(2, E), v(2, E, W), v(2, R, E), v(2, E), v(2, N, E), v(2, E),
            pltpu.SemaphoreType.DMA((10,)),
            v(B, T, W), v(B, T, W), v(B, T, W), v(8, E), v(8, E), v(8, E), v(8, E), v(8, E), v(8, E),
            v(L + 6, C, E), v(L + 6, C, E),
            v(2, T, E), v(2, T, E), v(2, T, W), v(2, 3, 32, W), v(2, 32, W), v(2, T, W),
            v(2, T, W), v(2, 3, 32, W), v(2, 32, W), v(2, T, W),
            v(2, T, E), v(2, T, E), v(2, T, E), v(T, E), v(2, N, C, E), v(2, T, 2 * N * W),
            pltpu.VMEM((2 * W, 2 * N * W), jnp.bfloat16),
            v(2, L, N, C, E), v(2, 32, 64, W), v(2, 32, 64, W), v(32, 64, W), v(32, 64, W),
            v(2, 32, 16, W), v(2, 32, 16, W), v(2, C, W), v(2, C, W), v(2, 32, C, W), v(2, 32, C, W),
            v(L + 1, 8, C, 3 * W), v(T, N * W), v(T, N * W), pltpu.VMEM((2 * N * W, W), jnp.bfloat16), v(T, E), v(T, E), v(T, E), v(W, E), v(T, E),
            v(4, E, W), v(4, 384, W), v(4, 384, W), v(4, 15, 24, W), v(4, 24, W), v(4, 24, W), v(4, 24, W),
            v(4, 384, W), v(4, 384, W),
            pltpu.SemaphoreType.DMA((copies,)),
            pltpu.SemaphoreType.DMA((copies,)),
        ],
        compiler_params=pltpu.CompilerParams(
            collective_id=0, has_side_effects=True, vmem_limit_bytes=LIMIT
        ),
        name="block",
    )(*args)
    return pl.pallas_call(
        store_kernel,
        out_shape=shapes,
        in_specs=[VM] * 5,
        out_specs=(hbm,) * 5,
        scratch_shapes=[pltpu.SemaphoreType.DMA((5,))],
        compiler_params=pltpu.CompilerParams(vmem_limit_bytes=1 << 20),
        name="store",
    )(*results)


def solution(mesh):
    row = P("ctx", "ch")
    in_specs = (
        row,
        row,
        row,
        P(None, None, "ch"),
        P(None, "ch"),
        P(None, "ch", None),
        P(None, None, "ch"),
        P(None, "ch"),
        P(None, None, "ch"),
        P(None, "ch"),
    )
    out_specs = (row, row, row, P(None, "ch", None), P(None, None, "ch"))
    return jax.shard_map(on_device, mesh=mesh, in_specs=in_specs, out_specs=out_specs, check_vma=False)
```

```python
import jax
import jax.numpy as jnp
from jax import lax
from jax.experimental import pallas as pl
from jax.experimental.pallas import tpu as pltpu
from jax.sharding import PartitionSpec as P

F32 = jnp.float32
MESH = pl.DeviceIdType.MESH

T = 128
C = 8
L = 16
E = 768
N = 16
R = 96
W = 128
B = E // W
TILES = 64

VM = pl.BlockSpec(memory_space=pltpu.VMEM)


def sds(*shape):
    return jax.ShapeDtypeStruct(shape, F32)


LOG2E = 1.4426950408889634
LN2 = 0.6931471805599453


def sigmoid(v):
    return 1.0 / (1.0 + jnp.exp(-v))


def softplus(v):
    return jnp.maximum(v, 0.0) + jnp.log1p(jnp.exp(-jnp.abs(v)))


def rows8(i):
    return pl.ds(pl.multiple_of(i * 8, 8), 8)


def parts(a):
    high = a.astype(jnp.bfloat16)
    return high, (a - high.astype(F32)).astype(jnp.bfloat16)


def product(a, b, left, right):
    (ah, al), (bh, bl) = parts(a), parts(b)

    def dot(u, v):
        return lax.dot_general(u, v, (((left,), (right,)), ((), ())), preferred_element_type=F32)

    return dot(ah, bh) + (dot(ah, bl) + dot(al, bh))


def nn(a, b):
    return product(a, b, 1, 0)


def nt(a, b):
    return product(a, b, 1, 1)


def tn(a, b):
    return product(a, b, 0, 0)


class Links:
    def __init__(self, send, recv):
        self.send, self.recv, self.used = send, recv, 0
        self.all = []

    def start(self, src, dst, device):
        k = self.used
        self.used += 1
        copy = pltpu.make_async_remote_copy(
            src_ref=src,
            dst_ref=dst,
            send_sem=self.send.at[k],
            recv_sem=self.recv.at[k],
            device_id=device,
            device_id_type=MESH,
        )
        copy.start()
        self.all.append(copy)
        return copy

    def finish(self):
        for copy in self.all:
            copy.wait_send()


def arrived(copies):
    for copy in copies:
        copy.wait_recv()


def hail(devices):
    barrier = pltpu.get_barrier_semaphore()
    for device in devices:
        pl.semaphore_signal(barrier, inc=1, device_id=device, device_id_type=MESH)
    return lambda: pl.semaphore_wait(barrier, len(devices))


def plus(a, p, n):
    return lax.rem(a + p, n)


def fill_edges(ext, prev, nxt, has_prev, has_next):
    sub = lax.broadcasted_iota(jnp.int32, (C, E), 0)
    for k in range(3):
        last = ext[3 + L - 3 + k]
        row = jnp.broadcast_to(prev[k : k + 1], (C, E))
        row = jnp.where(has_prev, row, 0.0)
        ext[k] = jnp.where(sub == 0, row, pltpu.roll(last, 1, 0))
        first = ext[3 + k]
        row = jnp.broadcast_to(nxt[k : k + 1], (C, E))
        row = jnp.where(has_next, row, 0.0)
        ext[3 + L + k] = jnp.where(sub == C - 1, row, pltpu.roll(first, C - 1, 0))


def by_lanes(src, dst):
    for b in range(B):
        dst[b] = src[:, b * W : (b + 1) * W]


def every(i):
    return pl.ds(i, C, stride=L)


def rows(k, n):
    return pl.ds(pl.multiple_of(k * n, 8), n)


class ChannelSum:
    def __init__(self, links, part, landed, own, total, me, ctx):
        self.links, self.part, self.landed, self.own, self.total = links, part, landed, own, total
        self.me, self.peers = me, [(ctx, plus(me, p, 4)) for p in range(1, 4)]

    def scatter(self):
        self.copies = [
            self.links.start(self.part.at[rows(peer[1], 32)], self.landed.at[p], peer)
            for p, peer in enumerate(self.peers)
        ]

    def gather(self):
        arrived(self.copies)
        mine = rows(self.me, 32)
        value = self.part[mine] + self.landed[0] + self.landed[1] + self.landed[2]
        self.own[...] = value
        self.total[mine] = value
        self.copies = [self.links.start(self.own, self.total.at[mine], peer) for peer in self.peers]

    def wait(self):
        arrived(self.copies)


class TileSum:
    def __init__(self, links, place, src, r0, t0, r1, t2, r3, t3, t4, fin):
        self.links, self.place, self.src = links, place, src
        self.r0, self.t0, self.r1, self.t2, self.r3, self.t3, self.t4, self.fin = r0, t0, r1, t2, r3, t3, t4, fin

    def core(self):
        self.copies = [self.links.start(self.src.at[rows(1 - self.place.core, 384)], self.r0, self.place.mate)]

    def scatter(self):
        arrived(self.copies)
        self.t0[...] = self.src[rows(self.place.core, 384)] + self.r0[...]
        self.copies = [
            self.links.start(self.t0.at[rows(k, 24)], self.r1.at[p], dev)
            for p, (k, dev) in enumerate(self.place.plane)
        ]

    def far(self):
        arrived(self.copies)
        v = self.t0[rows(self.place.k, 24)]
        for p in range(15):
            v = v + self.r1[p]
        self.t2[...] = v
        self.copies = [self.links.start(self.t2, self.r3, self.place.far)]

    def gather(self):
        arrived(self.copies)
        v = self.t2[...] + self.r3[...]
        mine = rows(self.place.k, 24)
        self.t3[...] = v
        self.t4[mine] = v
        self.copies = [self.links.start(self.t3, self.t4.at[mine], dev) for _, dev in self.place.plane]

    def join(self):
        arrived(self.copies)
        self.copies = [self.links.start(self.t4, self.fin, self.place.mate)]

    def end(self, write):
        write(self.place.core, self.t4)
        arrived(self.copies)
        write(1 - self.place.core, self.fin)


class Place:
    def __init__(self):
        ctx, me = lax.axis_index("ctx"), lax.axis_index("ch")
        self.ctx, self.me = ctx, me
        self.after, self.before = (plus(ctx, 1, TILES), me), (plus(ctx, TILES - 1, TILES), me)
        self.core, self.y, self.x = lax.rem(ctx, 2), lax.rem(ctx // 2, 4), lax.rem(ctx // 8, 4)
        self.z = ctx // 32
        self.mate = (ctx - self.core + 1 - self.core, me)
        self.far = (lax.rem(ctx + 32, TILES), me)
        self.k = self.x * 4 + self.y
        self.plane = []
        for dx in range(4):
            for dy in range(4):
                if dx or dy:
                    x, y = plus(self.x, dx, 4), plus(self.y, dy, 4)
                    self.plane.append((x * 4 + y, (ctx + (x - self.x) * 8 + (y - self.y) * 2, me)))
        self.k32 = lax.rem(ctx, 32)
        base = ctx - self.k32
        self.half = [(k, (base + k, me)) for k in [plus(self.k32, p, 32) for p in range(1, 32)]]
        self.ch = [(ctx, plus(me, p, 4)) for p in range(1, 4)]

    def everyone(self):
        return [self.after, self.before, self.far] + [dev for _, dev in self.half] + self.ch


class Carries:
    def __init__(self, links, place, d, msg, r1, zs, zr, out, rc):
        self.links, self.place, self.d = links, place, d
        self.msg, self.r1, self.zs, self.zr, self.out, self.rc = msg, r1, zs, zr, out, rc

    def pick(self, up, down):
        sub = lax.broadcasted_iota(jnp.int32, (C, W), 0)
        return jnp.where(sub < 3, up, down) if self.d == 0 else jnp.where(sub < 3, down, up)

    def start(self):
        me = self.place.k32
        self.copies = [self.links.start(self.msg.at[k], self.r1.at[me], dev) for k, dev in self.place.half]
        self.r1[me] = self.msg[me]

    def far(self):
        arrived(self.copies)
        r1 = self.r1
        u = dn = jnp.zeros((C, W), F32)
        for s in range(32):
            u = r1[s, 8:16] * u + r1[s, 0:8]
            dn = r1[31 - s, 8:16] * dn + r1[31 - s, 0:8]
        self.zs[...] = self.pick(u, dn)
        self.copies = [self.links.start(self.zs, self.zr, self.place.far)]

    def back(self):
        arrived(self.copies)
        got, z, r1, out = self.zr[...], self.place.z, self.r1, self.out
        u, dn = jnp.where(z == 1, got, 0.0), jnp.where(z == 0, got, 0.0)
        ups, downs = [], []
        for s in range(32):
            ups.append(u)
            u = r1[s, 8:16] * u + r1[s, 0:8]
            if s < 16:
                out[s] = ups[s]
            downs.append(dn)
            dn = r1[31 - s, 8:16] * dn + r1[31 - s, 0:8]
            if s < 16:
                out[31 - s] = downs[s]
            else:
                out[s] = self.pick(ups[s], out[s])
                out[31 - s] = self.pick(out[31 - s], downs[s])
        me = self.place.k32
        self.copies = [self.links.start(out.at[k], self.rc.at[me], dev) for k, dev in self.place.half]
        self.rc[me] = out[me]

    def wait(self):
        arrived(self.copies)


def block_kernel(
    tok_h, gate_h, cot_h, cw_h, cb_h, sw_h, stw_h, stb_h, dl_h, skip_h,
    out_o, tg_o, gg_o, selg_o, stepg_o,
    tok, gate, cot, cw, cb, sw, stw, stb, dl, skip, in_sem,
    tiles, gates, cots, prev, nxt, prev2, nxt2, send0, send1, ext0, ext1,
    act, sg, part, landed, own, proj, part2, landed2, own2, gp,
    pre, step, drv, g, rt, base, lift, dec, ca, cp, su, sd,
    msg, cr1, czs, czr, cout, crc,
    ss, go, gi, pick, ya, dg, stt, wpad, tgp,
    w_src, w_r0, w_t0, w_r1, w_t2, w_r3, w_t3, w_t4, w_fin,
    send, recv,
):
    pairs = (
        (tok_h, tok), (cw_h, cw), (cb_h, cb), (gate_h, gate), (cot_h, cot), (dl_h, dl),
        (sw_h, sw), (stw_h, stw), (stb_h, stb), (skip_h, skip),
    )
    loads = [pltpu.make_async_copy(a, b, in_sem.at[k]) for k, (a, b) in enumerate(pairs)]
    for load in loads:
        load.start()
    place = Place()
    ctx, me = place.ctx, place.me
    meet = hail(place.everyone())
    meet()
    links = Links(send, recv)
    halo = [
        links.start(tok_h.at[pl.ds(T - 8, 8)], prev, place.after),
        links.start(tok_h.at[pl.ds(0, 8)], nxt, place.before),
    ]
    for load in loads[:3]:
        load.wait()
    by_lanes(tok, tiles)
    for i in range(L):
        for b in range(B):
            ext0[3 + i, :, b * W : (b + 1) * W] = tiles[b, every(i)]

    def conv(d):
        def one(i, carry):
            v = jnp.broadcast_to(cb[d : d + 1], (C, E))
            for k in range(4):
                v = v + cw[d, k : k + 1] * ext0[i + (k if d == 0 else 6 - k)]
            s = sigmoid(v)
            act[d, rows8(i)] = v * s
            sg[d, rows8(i)] = s * (1.0 + v * (1.0 - s))
            return carry

        return one

    lax.fori_loop(3, L, conv(0), 0)
    lax.fori_loop(0, L - 3, conv(1), 0)
    for load in loads[3:]:
        load.wait()
    by_lanes(gate, gates)
    by_lanes(cot, cots)

    def gated(i, carry):
        for b in range(B):
            v = gates[b, every(i)]
            g[rows8(i), b * W : (b + 1) * W] = cots[b, every(i)] * v * sigmoid(v)
        return carry

    lax.fori_loop(0, L, gated, 0, unroll=2)
    for d in range(2):
        ca[d, :, 48:64] = jnp.zeros((32, 16, W), F32)
        cp[d, :, 48:64] = jnp.zeros((32, 16, W), F32)
        for n in range(N):
            rt[d, n] = jnp.broadcast_to(-jnp.exp(dl[d, n : n + 1]) * LOG2E, (C, E))
    lane = lax.broadcasted_iota(jnp.int32, (W, W), 1)
    line = lax.broadcasted_iota(jnp.int32, (W, W), 0)
    for n in range(2 * N):
        at = pl.ds(n * W, W)
        pick[at] = jnp.where(lane == R + n, 1.0, 0.0).astype(jnp.bfloat16)
        lift[0:W, at] = jnp.where(line == R + n, 1.0, 0.0).astype(jnp.bfloat16)
        lift[W : 2 * W, at] = jnp.where(line == R + n, 1.0, 0.0).astype(jnp.bfloat16)
    arrived(halo)
    fill_edges(ext0, prev[5:8], nxt[0:3], ctx > 0, ctx < TILES - 1)
    sums = [ChannelSum(links, part.at[d], landed.at[d], own.at[d], proj.at[d], me, ctx) for d in range(2)]
    lax.fori_loop(0, 3, conv(0), 0)
    part[0] = nn(act[0], sw[0])
    sums[0].scatter()
    lax.fori_loop(L - 3, L, conv(1), 0)
    part[1] = nn(act[1], sw[1])
    sums[1].scatter()
    for d in range(2):
        sums[d].gather()
    def basis(d, i, n):
        return base[d, rows8(i), n * W : (n + 1) * W]

    H = 8
    carries = [Carries(links, place, d, *[r.at[d] for r in (msg, cr1, czs, czr, cout, crc)]) for d in range(2)]
    for d in range(2):
        sums[d].wait()
        spread = jnp.concatenate(parts(proj[d]), axis=1)
        for n in range(0, 2 * N, 2):
            at = pl.ds(n * W, 2 * W)
            base[d, :, at] = jnp.dot(spread, lift[:, at], preferred_element_type=F32)
        pre[d] = nn(proj[d][:, :R], stw[d]) + stb[d : d + 1]

        def prepare(i, carry, d=d):
            st = softplus(pre[d, rows8(i)])
            step[d, rows8(i)] = st
            drv[d, rows8(i)] = st * act[d, rows8(i)]
            return carry

        lax.fori_loop(0, L, prepare, 0, unroll=PREP)
        for half in range(N // H):

            def ends(c, carry, d=d, half=half):
                lanes = pl.ds(pl.multiple_of(c * W, W), W)

                def advance(i, state):
                    f, p, a = state
                    ii = i if d == 0 else L - 1 - i
                    st, dr = step[d, rows8(ii), lanes], drv[d, rows8(ii), lanes]
                    gg = g[rows8(ii), lanes]
                    nf, np_, na = [], [], []
                    for j in range(H):
                        n = half * H + j
                        e = jnp.exp2(st * rt[d, n, :, lanes])
                        dec[d, ii, n, :, lanes] = e
                        nf.append(e * f[j] + basis(d, ii, n) * dr)
                        v = p[j] * e
                        np_.append(v)
                        na.append(a[j] + v * (basis(d, ii, N + n) * gg))
                    return nf, np_, na

                zero = [jnp.zeros((C, W), F32)] * H
                f, p, a = lax.fori_loop(0, L, advance, (zero, [jnp.ones((C, W), F32)] * H, zero), unroll=UNROLL[d])
                for j in range(H):
                    n = half * H + j
                    slot = n * 2 + c // 3
                    first, second = rows8(lax.rem(c, 3)), rows8(lax.rem(c, 3) + 3)
                    ca[d, slot, first] = f[j]
                    ca[d, slot, second] = a[j]
                    cp[d, slot, first] = p[j]
                    cp[d, slot, second] = p[j]
                return carry

            lax.fori_loop(0, B, ends, 0)

        def totals(q, carry, d=d):
            u = dn = jnp.zeros((C, W), F32)
            pt = jnp.ones((C, W), F32)
            for s in range(C):
                p, back = cp[d, q, pl.ds(s, C, stride=C)], pl.ds(C - 1 - s, C, stride=C)
                u = p * u + ca[d, q, pl.ds(s, C, stride=C)]
                pt = pt * p
                dn = cp[d, q, back] * dn + ca[d, q, back]
            msg[d, q, 0:8] = carries[d].pick(u, dn)
            msg[d, q, 8:16] = pt
            return carry

        lax.fori_loop(0, 32, totals, 0, unroll=4)
        if d == 0:
            carries[0].start()
    carries[1].start()
    carries[0].far()
    carries[0].back()
    carries[1].far()
    carries[0].wait()
    carries[1].back()

    Q = 3
    QW = Q * W

    def folded(v):
        r = v[:, :W]
        for k in range(1, Q):
            r = r + v[:, k * W : (k + 1) * W]
        return r

    def wide(v):
        return jnp.concatenate([v] * Q, axis=1)

    def begin(src, first, half, cb, j):
        n = half * H + j
        return jnp.concatenate([src[n * 2 + cb, pl.ds((first + k) * 8, 8)] for k in range(Q)], axis=1)

    blocks = [(half, cb) for half in range(N // H) for cb in range(B // Q)]

    def sweep(d, between):
        def starts(q, carry):
            u = dn = crc[d, q]
            for s in range(C):
                at, back = pl.ds(s, C, stride=C), pl.ds(C - 1 - s, C, stride=C)
                su[q, at] = u
                u = cp[d, q, at] * u + ca[d, q, at]
                sd[q, back] = dn
                dn = cp[d, q, back] * dn + ca[d, q, back]
            return carry

        lax.fori_loop(0, 32, starts, 0, unroll=4)
        fs, bs = (su, sd) if d == 0 else (sd, su)
        for half, cb in blocks:
            for step_on in between.get((half, cb), ()):
                step_on()
            lanes = pl.ds(cb * QW, QW)

            def forward(i, state, half=half, cb=cb, lanes=lanes):
                ii = i if d == 0 else L - 1 - i
                dr, gg = drv[d, rows8(ii), lanes], g[rows8(ii), lanes]
                if half == 0:
                    y = skip[d : d + 1, lanes] * act[d, rows8(ii), lanes]
                    if d == 1:
                        y = y + ya[rows8(ii), lanes]
                else:
                    y = ya[rows8(ii), lanes]
                new = []
                for j in range(H):
                    n = half * H + j
                    s = dec[d, ii, n, :, lanes] * state[j] + wide(basis(d, ii, n)) * dr
                    y = y + wide(basis(d, ii, N + n)) * s
                    v, at = folded(s * gg), pl.ds(n * W, W)
                    go[rows8(ii), at] = v if cb == 0 else go[rows8(ii), at] + v
                    ss[i + 1, j] = s
                    new.append(s)
                ya[rows8(ii), lanes] = y
                return new

            first = [begin(fs, 0, half, cb, j) for j in range(H)]
            for j in range(H):
                ss[0, j] = first[j]
            lax.fori_loop(0, L, forward, first, unroll=SW)

            def retreat(t, carried, half=half, cb=cb, lanes=lanes):
                i = L - 1 - t
                ii = i if d == 0 else L - 1 - i
                dr, gg = drv[d, rows8(ii), lanes], g[rows8(ii), lanes]
                if half == 0:
                    a1 = a2 = jnp.zeros((C, QW), F32)
                else:
                    a1, a2 = stt[rows8(ii), lanes], dg[rows8(ii), lanes]
                new = []
                for j in range(H):
                    n = half * H + j
                    adj = carried[j] + wide(basis(d, ii, N + n)) * gg
                    back = dec[d, ii, n, :, lanes] * adj
                    a1 = a1 + (back * ss[i, j]) * rt[d, n, :, lanes]
                    a2 = a2 + adj * wide(basis(d, ii, n))
                    v, at = folded(adj * dr), pl.ds(n * W, W)
                    gi[rows8(ii), at] = v if cb == 0 else gi[rows8(ii), at] + v
                    new.append(back)
                stt[rows8(ii), lanes] = a1
                dg[rows8(ii), lanes] = a2
                return new

            lax.fori_loop(0, L, retreat, [begin(bs, 3, half, cb, j) for j in range(H)], unroll=SW)

        def close(i, carry):
            at = rows8(i)
            slope = dg[at]
            ga = g[at] * skip[d : d + 1] + slope * step[d, at]
            stt[at] = (stt[at] * LN2 + slope * act[d, at]) * sigmoid(pre[d, at])
            drv[d, at] = ga
            return carry

        lax.fori_loop(0, L, close, 0)
        wpad[0:R] = stw[d]
        part2[d] = nt(stt[...], wpad[...])

        total = part2[d]
        for k in range(0, 2 * N, 4):
            source = (gi if k < N else go)[:, (k % N) * W : (k % N + 4) * W]
            for half in parts(source):
                total = total + jnp.dot(half, pick[k * W : (k + 4) * W], preferred_element_type=F32)
        part2[d] = total

    wpad[...] = jnp.zeros_like(wpad)
    back_sums = [ChannelSum(links, part2.at[d], landed2.at[d], own2.at[d], gp.at[d], me, ctx) for d in range(2)]
    weights = [
        TileSum(links, place, *[r.at[k] for r in (w_src, w_r0, w_t0, w_r1, w_t2, w_r3, w_t3, w_t4, w_fin)])
        for k in range(4)
    ]
    s0, s1, t0, t1 = weights

    def step_part(d, stream):
        v = tn(proj[d], stt[...])
        for b in range(B):
            stream.src[b * W : (b + 1) * W] = v[:, b * W : (b + 1) * W]

    def select_part(d, stream, ext):
        stream.src[...] = tn(act[d], gp[d])
        stream.core()
        tgp[...] = nt(gp[d], sw[d])

        def conv_grad(i, carry):
            ext[3 + i] = (drv[d, rows8(i)] + tgp[rows8(i)]) * sg[d, rows8(i)]
            return carry

        lax.fori_loop(0, L, conv_grad, 0)

    def step_end(d):
        def write(core, src):
            for b in range(3):
                lanes = pl.ds(pl.multiple_of(core * 384 + b * W, W), W)
                stepg_o[d, :, lanes] = src[b * W : b * W + R]

        return write

    def select_end(d):
        def write(core, src):
            selg_o[d, rows(core, 384)] = src[...]

        return write

    sweep(0, {})
    back_sums[0].scatter()
    step_part(0, s0)
    s0.core()
    carries[1].wait()
    sweep(1, {(1, 0): [back_sums[0].gather, s0.scatter]})
    back_sums[1].scatter()
    step_part(1, s1)
    s1.core()
    back_sums[0].wait()
    select_part(0, t0, ext0)
    s0.far()
    back_sums[1].gather()
    s0.gather()
    s1.scatter()
    t0.scatter()

    def gates_back(i, carry):
        for b in range(B):
            v, ct, y = gates[b, every(i)], cots[b, every(i)], ya[rows8(i), b * W : (b + 1) * W]
            s = sigmoid(v)
            gates[b, every(i)] = y * v * s
            cots[b, every(i)] = ct * y * (s * (1.0 + v * (1.0 - s)))
        return carry

    lax.fori_loop(0, L, gates_back, 0, unroll=2)
    for b in range(B):
        out_o[:, b * W : (b + 1) * W] = gates[b]
        gg_o[:, b * W : (b + 1) * W] = cots[b]
    back_sums[1].wait()
    select_part(1, t1, ext1)
    for k in range(3):
        send0[k : k + 1] = ext0[3 + k, 0:1]
        send1[k : k + 1] = ext1[3 + L - 3 + k, C - 1 : C]
    halo = [links.start(send0, nxt2, place.before), links.start(send1, prev2, place.after)]
    t1.scatter()
    s1.far()
    t0.far()
    s0.join()

    t1.far()
    s1.gather()
    t0.gather()
    arrived(halo)
    fill_edges(ext0, prev2[0:3], nxt2[0:3], ctx > 0, ctx < TILES - 1)
    fill_edges(ext1, prev2[0:3], nxt2[0:3], ctx > 0, ctx < TILES - 1)

    def conv_back(i, carry):
        v = jnp.zeros((C, E), F32)
        for k in range(4):
            v = v + cw[0, k : k + 1] * ext0[i + 6 - k] + cw[1, k : k + 1] * ext1[i + k]
        for b in range(B):
            tiles[b, every(i)] = v[:, b * W : (b + 1) * W]
        return carry

    lax.fori_loop(0, L, conv_back, 0)
    for b in range(B):
        tg_o[:, b * W : (b + 1) * W] = tiles[b]
    t1.gather()
    s1.join()
    t0.join()
    s0.end(step_end(0))
    t1.join()
    s1.end(step_end(1))
    t0.end(select_end(0))
    t1.end(select_end(1))
    links.finish()


UNROLL = (8, 4)
PREP = 2
SW = 2
LIMIT = 49 << 20


def store_kernel(*refs):
    ins, outs, sem = refs[:5], refs[5:10], refs[10]
    copies = [pltpu.make_async_copy(a, b, sem.at[k]) for k, (a, b) in enumerate(zip(ins, outs))]
    for copy in copies:
        copy.start()
    for copy in copies:
        copy.wait()


def on_device(*args):
    v = lambda *shape: pltpu.VMEM(shape, F32)
    copies = 2 + 12 + 2 * 63 + 12 + 2 + 4 * 33
    hbm = pl.BlockSpec(memory_space=pltpu.HBM)
    shapes = (sds(T, E), sds(T, E), sds(T, E), sds(2, E, W), sds(2, R, E))
    args = [pltpu.with_memory_space_constraint(a, pltpu.HBM) for a in args]
    results = pl.pallas_call(
        block_kernel,
        out_shape=shapes,
        in_specs=[hbm] * 10,
        out_specs=(VM,) * 5,
        scratch_shapes=[
            v(T, E), v(T, E), v(T, E), v(2, 4, E), v(2, E), v(2, E, W), v(2, R, E), v(2, E), v(2, N, E), v(2, E),
            pltpu.SemaphoreType.DMA((10,)),
            v(B, T, W), v(B, T, W), v(B, T, W), v(8, E), v(8, E), v(8, E), v(8, E), v(8, E), v(8, E),
            v(L + 6, C, E), v(L + 6, C, E),
            v(2, T, E), v(2, T, E), v(2, T, W), v(2, 3, 32, W), v(2, 32, W), v(2, T, W),
            v(2, T, W), v(2, 3, 32, W), v(2, 32, W), v(2, T, W),
            v(2, T, E), v(2, T, E), v(2, T, E), v(T, E), v(2, N, C, E), v(2, T, 2 * N * W),
            pltpu.VMEM((2 * W, 2 * N * W), jnp.bfloat16),
            v(2, L, N, C, E), v(2, 32, 64, W), v(2, 32, 64, W), v(32, 64, W), v(32, 64, W),
            v(2, 32, 16, W), v(2, 32, 16, W), v(2, C, W), v(2, C, W), v(2, 32, C, W), v(2, 32, C, W),
            v(L + 1, 8, C, 3 * W), v(T, N * W), v(T, N * W), pltpu.VMEM((2 * N * W, W), jnp.bfloat16), v(T, E), v(T, E), v(T, E), v(W, E), v(T, E),
            v(4, E, W), v(4, 384, W), v(4, 384, W), v(4, 15, 24, W), v(4, 24, W), v(4, 24, W), v(4, 24, W),
            v(4, 384, W), v(4, 384, W),
            pltpu.SemaphoreType.DMA((copies,)),
            pltpu.SemaphoreType.DMA((copies,)),
        ],
        compiler_params=pltpu.CompilerParams(
            collective_id=0, has_side_effects=True, vmem_limit_bytes=LIMIT
        ),
        name="block",
    )(*args)
    return pl.pallas_call(
        store_kernel,
        out_shape=shapes,
        in_specs=[VM] * 5,
        out_specs=(hbm,) * 5,
        scratch_shapes=[pltpu.SemaphoreType.DMA((5,))],
        compiler_params=pltpu.CompilerParams(vmem_limit_bytes=1 << 20),
        name="store",
    )(*results)


def solution(mesh):
    row = P("ctx", "ch")
    in_specs = (
        row,
        row,
        row,
        P(None, None, "ch"),
        P(None, "ch"),
        P(None, "ch", None),
        P(None, None, "ch"),
        P(None, "ch"),
        P(None, None, "ch"),
        P(None, "ch"),
    )
    out_specs = (row, row, row, P(None, "ch", None), P(None, None, "ch"))
    return jax.shard_map(on_device, mesh=mesh, in_specs=in_specs, out_specs=out_specs, check_vma=False)
```
